32 devices in a mesh: dp: 8 (over y, x, core), table: 4 (over z).
Axes of the slice: x: 2, y: 2, z: 4, core: 2. Of those that a mesh axis runs over, the one named last changes fastest.
Arguments:
- item_ids: int32 [64, 384], P(('dp', 'table')), may hold values from 0 to 393215, as said below
- table_ids: int32 [64, 384], P(('dp', 'table')), may hold values from 0 to 3
- lengths: int32 [64], P(('dp', 'table')), may hold values from 24 to 384
- assignment: int32 [64], P(('dp', 'table')), may hold values from 0 to 63, as said below
- table_a: bfloat16 [393216, 64], P(('dp', 'table')), may hold values from -6 to 6
- table_b: bfloat16 [393216, 64], P(('dp', 'table')), may hold values from -6 to 6
- table_c: bfloat16 [196608, 128], P(('dp', 'table')), may hold values from -6 to 6
- table_d: bfloat16 [65536, 256], P(('dp', 'table')), may hold values from -6 to 6
- proj_weight: bfloat16 [512, 512], P('dp'), may hold values from -0.5 to 0.5
- in_weight: bfloat16 [512, 2048], P('dp'), may hold values from -0.25 to 0.25
- out_weight: bfloat16 [512, 512], P('dp'), may hold values from -0.25 to 0.25
- cotangent: bfloat16 [64, 384, 512], P(('dp', 'table')), may hold values from -6 to 6
Outputs:
- output: bfloat16 [64, 384, 512], P(('dp', 'table'))
- grad_a: bfloat16 [393216, 64], P(('dp', 'table'))
- grad_b: bfloat16 [393216, 64], P(('dp', 'table'))
- grad_c: bfloat16 [196608, 128], P(('dp', 'table'))
- grad_d: bfloat16 [65536, 256], P(('dp', 'table'))
- grad_proj: float32 [512, 512], P('dp')
- grad_in: float32 [512, 2048], P('dp')
- grad_out: float32 [512, 512], P('dp')
The draws below stay inside these ranges and needn't reach their ends.
Inputs may be any that keep to these rules, and one draw needn't show every extreme that they name: `item_ids`: A sequence's events past its length name rows too. An event's item is below 32 times the rows one device holds of the event's table (row r of a table lies on device r // (rows a device of that table) along dp+table). After the move, the events of the 2 slots of one device name at most 12 times rows of one table held by one device, and for some table and device exactly 12 times, from every device. `assignment`: A permutation of the sequence slots; a sequence moves only among the devices of its own table index, and each device receives 2 sequences.
All inputs are finite; a program needn't handle non-finite values.
Results may differ from the reference program's by a relative error of at most 0.028.
Values may be sent and summed in bfloat16 or wider, within the bound.
No kernel may reach another device: no remote copies, remote signals or barrier semaphores. Data moves between devices by JAX's collectives and lax.ppermute only.
A program may use at most 128 MiB of HBM per device.

```python
import jax
import jax.numpy as jnp
from jax import lax

D = 512
HEADS = 4
FF = 2048
WIDTH_A = 64
WIDTH_B = 64
WIDTH_C = 128
WIDTH_D = 256
WSUM = 512
ROWS_A = 12288
ROWS_B = 12288
ROWS_C = 6144
ROWS_D = 2048
MAXLEN = 384
SEQ_DEV = 2
SEQS = 64
CAP = 12
TROWS_A = 393216
TROWS_B = 393216
TROWS_C = 196608
TROWS_D = 65536
N_DP = 8
N_TABLE = 4
DEVICES = 32


def build_layout(key):
    base = jax.random.fold_in(key, 4242)
    subkeys = jax.random.split(base, 5)
    seq_total = SEQ_DEV * DEVICES
    tok_total = SEQ_DEV * MAXLEN
    seq_index = jnp.arange(seq_total, dtype=jnp.int32)
    seq_lengths = jax.random.randint(subkeys[0], (seq_total,), MAXLEN // 16, MAXLEN + 1, dtype=jnp.int32)
    group_of = seq_index // SEQ_DEV % N_TABLE
    sort_key = group_of * ((MAXLEN + 2) * seq_total) + (MAXLEN + 1 - seq_lengths) * seq_total + seq_index
    ordering = jnp.argsort(sort_key)
    seq_rank = jnp.zeros((seq_total,), jnp.int32).at[ordering].set(seq_index)
    in_group = seq_rank - group_of * (N_DP * SEQ_DEV)
    rounds = in_group // N_DP
    position = in_group % N_DP
    device_of = jnp.where(rounds % 2 == 0, position, N_DP - 1 - position)
    targets = (device_of * N_TABLE + group_of) * SEQ_DEV + rounds
    slot_total = 4 * DEVICES * CAP
    bucket = jnp.arange(slot_total, dtype=jnp.int32) // CAP
    special = jax.random.randint(subkeys[1], (), 0, 4 * DEVICES, dtype=jnp.int32)
    noise_bits = jax.random.randint(subkeys[2], (DEVICES, slot_total), 0, (1 << 30) // slot_total, dtype=jnp.int32)
    scores = jnp.where(bucket[None, :] == special, -slot_total, noise_bits * slot_total) + jnp.arange(slot_total, dtype=jnp.int32)[None, :]
    picked = jnp.argsort(scores, axis=1)[:, :tok_total]
    chosen = bucket[picked]
    shuffle_bits = jax.random.randint(subkeys[3], (DEVICES, tok_total), 0, (1 << 30) // tok_total, dtype=jnp.int32)
    shuffle = jnp.argsort(shuffle_bits * tok_total + jnp.arange(tok_total, dtype=jnp.int32)[None, :], axis=1)
    chosen = jnp.take_along_axis(chosen, shuffle, axis=1)
    table_of = chosen % 4
    owners = chosen // 4
    row_limit = jnp.where(table_of == 0, ROWS_A, jnp.where(table_of == 1, ROWS_B, jnp.where(table_of == 2, ROWS_C, ROWS_D)))
    local_row = jax.random.randint(subkeys[4], (DEVICES, tok_total), 0, 1 << 30, dtype=jnp.int32) % row_limit
    item_rows = (owners * row_limit + local_row).reshape(seq_total, MAXLEN)[targets]
    table_rows = table_of.reshape(seq_total, MAXLEN)[targets]
    return (seq_lengths, targets, item_rows, table_rows)


def draw_lengths(key, part):
    return build_layout(key)[0]


def draw_assignment(key, part):
    return build_layout(key)[1]


def draw_item_ids(key, part):
    return build_layout(key)[2]


def draw_table_ids(key, part):
    return build_layout(key)[3]


def strengthened(values, key, source, target, shards_of, factor):
    def block_of(axis_at):
        return (jnp.arange(values.shape[axis_at]) // (values.shape[axis_at] // shards_of)).reshape((-1,) + (1,) * (values.ndim - 1 - axis_at))

    one_side = jax.random.permutation(key, shards_of)[block_of(target)]
    second = (block_of(target) + shards_of // 2) % shards_of
    return jnp.where((block_of(source) == one_side) | (block_of(source) == second), factor * values, values)


def steps_of(own_key, dims, shards, smallest, largest):
    def one(axis_at, parts):
        heights = jax.random.uniform(jax.random.fold_in(jax.random.fold_in(own_key, 6), axis_at), (parts,), jnp.float32, smallest / len(shards), largest / len(shards))
        return jnp.repeat(jnp.exp(heights), dims[axis_at] // parts).reshape((-1,) + (1,) * (len(dims) - axis_at - 1))

    loudness = one(*shards[0])
    for cut in shards[1:]:
        loudness = loudness * one(*cut)
    return loudness


def normal_values(own_key, shape, width, limit, cuts=(), kind=jnp.bfloat16):
    loudness = steps_of(own_key, shape, cuts, -0.22, 0.18) if cuts else 1.0
    values = jax.random.normal(own_key, shape, jnp.float32) * width * loudness
    return jnp.minimum(jnp.maximum(values, -limit), limit).astype(kind)


def gaussian_with(rng, dims, scale, reach, cuts, heavy, kind=jnp.bfloat16):
    values = scale * jax.random.normal(rng, dims, jnp.float32)
    if cuts:
        values = values * steps_of(rng, dims, cuts, -0.22, 0.18)
    return jnp.clip(strengthened(values, jax.random.fold_in(rng, 3), *heavy), -reach, reach).astype(kind)


def setup_inputs(seed: int = 0) -> dict:
    splits = jax.random.split(jax.random.key(seed), 13)
    return {
        "item_ids": draw_item_ids(jax.random.fold_in(splits[12], 71), 0),
        "table_ids": draw_table_ids(jax.random.fold_in(splits[12], 71), 0),
        "lengths": draw_lengths(jax.random.fold_in(splits[12], 71), 0),
        "assignment": draw_assignment(jax.random.fold_in(splits[12], 71), 0),
        "table_a": normal_values(splits[4], (TROWS_A, WIDTH_A), 1.0, 6.0, ((0, 32),)),
        "table_b": normal_values(splits[5], (TROWS_B, WIDTH_B), 1.0, 6.0, ((0, 32),)),
        "table_c": normal_values(splits[6], (TROWS_C, WIDTH_C), 1.0, 6.0, ((0, 32),)),
        "table_d": normal_values(splits[7], (TROWS_D, WIDTH_D), 1.0, 6.0, ((0, 32),)),
        "proj_weight": normal_values(splits[8], (WSUM, D), (WSUM // 4) ** -0.5, 0.5, ((0, 8),)),
        "in_weight": normal_values(splits[9], (D, FF), D ** -0.5, 0.25, ((0, 8),)),
        "out_weight": normal_values(splits[10], (D, D), D ** -0.5, 0.25, ((0, 8),)),
        "cotangent": gaussian_with(splits[11], (SEQS, MAXLEN, D), 1.0, 6.0, ((0, 32),), (0, 2, 32, 2.75)),
    }


def normalize(values):
    centred = values - lax.optimization_barrier(jnp.mean(values, axis=-1, keepdims=True))
    return centred * lax.rsqrt(lax.optimization_barrier(jnp.mean(centred * centred, axis=-1, keepdims=True)) + 1e-05)

def hstu_layer(embedded, seq_lengths, in_full, out_full):
    seq_count, seq_span, model_width = embedded.shape
    head_dim = model_width // HEADS
    normed = normalize(embedded.astype(jnp.float32)).astype(jnp.bfloat16)
    projected = jnp.dot(normed.reshape(seq_count * seq_span, model_width), in_full, preferred_element_type=jnp.float32)
    activated = jax.nn.silu(projected).astype(jnp.bfloat16).reshape(seq_count, seq_span, 4, HEADS, head_dim)
    gate_part = activated[:, :, 0].reshape(seq_count, seq_span, model_width)
    value_part = activated[:, :, 1].astype(jnp.float32)
    query_part = activated[:, :, 2].astype(jnp.float32)
    key_part = activated[:, :, 3].astype(jnp.float32)
    scores = jnp.einsum('sihe,sjhe->shij', query_part, key_part) * head_dim ** (-0.5)
    position = jnp.arange(seq_span, dtype=jnp.int32)
    causal = (position[None, :] <= position[:, None])[None, None]
    inside = position[None, None, None, :] < seq_lengths[:, None, None, None]
    attn = jnp.where(causal & inside, jax.nn.silu(scores), 0.0).astype(jnp.bfloat16)
    attended = jnp.einsum('shij,sjhe->sihe', attn.astype(jnp.float32), value_part).reshape(seq_count, seq_span, model_width)
    gated_rows = (normalize(attended) * gate_part.astype(jnp.float32)).astype(jnp.bfloat16)
    branch = jnp.dot(gated_rows.reshape(seq_count * seq_span, model_width), out_full, preferred_element_type=jnp.float32)
    return (embedded.astype(jnp.float32) + branch.reshape(seq_count, seq_span, model_width)).astype(jnp.bfloat16)

def reference(item_ids, table_ids, lengths, assignment, table_a, table_b, table_c, table_d, proj_weight, in_weight, out_weight, cotangent):
    tables = (table_a, table_b, table_c, table_d)
    event_items = jnp.zeros_like(item_ids).at[assignment].set(item_ids).reshape(-1)
    event_tables = jnp.zeros_like(table_ids).at[assignment].set(table_ids).reshape(-1)
    seq_lengths = jnp.zeros_like(lengths).at[assignment].set(lengths)
    pieces = []
    for which in range(4):
        hit = event_tables == which
        fetched = tables[which][jnp.where(hit, event_items, 0)]
        pieces.append(jnp.where(hit[:, None], fetched, jnp.zeros((), jnp.bfloat16)))
    rows_cat = jnp.concatenate(pieces, axis=1)
    model_width = proj_weight.shape[1]
    embedded = jnp.dot(rows_cat, proj_weight, preferred_element_type=jnp.float32).astype(jnp.bfloat16)
    embedded = embedded.reshape(DEVICES, SEQ_DEV, MAXLEN, model_width)
    position = jnp.arange(MAXLEN, dtype=jnp.int32)
    valid = position[None, :] < seq_lengths[:, None]
    out_grad = jnp.where(valid[:, :, None], cotangent, jnp.zeros((), jnp.bfloat16)).reshape(DEVICES, SEQ_DEV, MAXLEN, model_width)
    block_lengths = seq_lengths.reshape(DEVICES, SEQ_DEV)

    def step(totals, block_data):
        embed_block, length_block, grad_block = block_data

        def apply_layer(values, first_weight, second_weight):
            return hstu_layer(values, length_block, first_weight, second_weight)
        result, backward = jax.vjp(apply_layer, embed_block, in_weight, out_weight)
        d_values, d_first, d_second = backward(grad_block)
        return ((totals[0] + d_first.astype(jnp.float32), totals[1] + d_second.astype(jnp.float32)), (result, d_values))
    start = (jnp.zeros(in_weight.shape, jnp.float32), jnp.zeros(out_weight.shape, jnp.float32))
    (grad_in, grad_out), (results, d_embedded) = lax.scan(step, start, (embedded, block_lengths, out_grad))
    output = results.reshape(DEVICES * SEQ_DEV, MAXLEN, model_width)
    d_flat = d_embedded.reshape(-1, model_width)
    d_rows = jnp.dot(d_flat, proj_weight.T, preferred_element_type=jnp.float32)
    grad_proj = jnp.dot(rows_cat.T, d_flat, preferred_element_type=jnp.float32)
    table_grads = []
    column = 0
    for which in range(4):
        row_total, row_width = tables[which].shape
        target = jnp.where(event_tables == which, event_items, row_total)
        summed = jnp.zeros((row_total, row_width), jnp.float32).at[target].add(d_rows[:, column:column + row_width], mode='drop')
        table_grads.append(summed.astype(jnp.bfloat16))
        column = column + row_width
    return (output, table_grads[0], table_grads[1], table_grads[2], table_grads[3], grad_proj, grad_in, grad_out)
```

```python
import functools

import jax
import jax.numpy as jnp
from jax import lax
from jax.experimental import pallas as pl
from jax.experimental.pallas import tpu as pltpu
from jax.sharding import PartitionSpec as P

HEADS = 4
SPLIT = 1024
F32 = jnp.float32
BF16 = jnp.bfloat16
NN = (((1,), (0,)), ((), ()))
NT = (((1,), (1,)), ((), ()))
TN = (((0,), (0,)), ((), ()))
VM = pl.BlockSpec(memory_space=pltpu.VMEM)
SM = pl.BlockSpec(memory_space=pltpu.SMEM)
HB = pl.BlockSpec(memory_space=pl.ANY)


def dot(left, right, dims=NN):
    return lax.dot_general(left, right, dims, preferred_element_type=F32)


def iota(shape, dim):
    return lax.broadcasted_iota(jnp.int32, shape, dim)


def onehot(flags):
    return jnp.where(flags, 1.0, 0.0).astype(BF16)


def floor_div(values, by):
    return jnp.floor((values.astype(F32) + 0.5) * (1.0 / by)).astype(jnp.int32)


def sigmoid(values):
    return 0.5 * jnp.tanh(0.5 * values) + 0.5


def log2(value):
    assert value & (value - 1) == 0
    return value.bit_length() - 1


def mask_of(index, seq):
    mask = 0
    for place, bit in enumerate(reversed(seq)):
        if (index >> place) & 1:
            mask |= 1 << bit
    return mask


def place_of(mask, seq):
    index = 0
    for place, bit in enumerate(reversed(seq)):
        index = index | (((mask >> bit) & 1) << place)
    return index


def owner_and_row(items, kinds, row_counts):
    rows = jnp.zeros_like(items)
    inverse = jnp.zeros(items.shape, F32)
    for which in range(4):
        hit = kinds == which
        rows = jnp.where(hit, row_counts[which], rows)
        inverse = jnp.where(hit, 1.0 / row_counts[which], inverse)
    owner = jnp.floor(items.astype(F32) * inverse).astype(jnp.int32)
    rest = items - owner * rows
    low = rest < 0
    owner = jnp.where(low, owner - 1, owner)
    rest = jnp.where(low, rest + rows, rest)
    high = rest >= rows
    owner = jnp.where(high, owner + 1, owner)
    rest = jnp.where(high, rest - rows, rest)
    return owner, rest


def plan_kernel(planes, devices, seq_count, span, capacity, row_counts, widths, *refs):
    me_ref, refs = refs[0], refs[1:]
    ids_refs, refs = refs[:planes], refs[planes:]
    table_refs, refs = refs[:4], refs[4:]
    send_ref, idxc_ref, idxr_ref, info_ref, infot_ref = refs[:5]
    held = refs[5:9]
    rows_scr, pack_scr, sems = refs[9:]
    copies = [pltpu.make_async_copy(table_refs[i], held[i], sems.at[i]) for i in range(4)]
    for copy in copies:
        copy.start()
    me = me_ref[0]
    seqs = devices * seq_count
    slots = devices * capacity
    toks = seq_count * span
    ids = jnp.concatenate([ref[...] for ref in ids_refs], axis=0)
    items = ids[:, :span]
    kinds = ids[:, span : 2 * span]
    tail = ids[:, 2 * span : 2 * span + 128]
    lens = tail[:, 0:1]
    target = tail[:, 1:2]
    own_items, own_kinds, own_valid = [], [], []
    for q in range(seq_count):
        hit = target == me * seq_count + q
        own_items.append(jnp.sum(jnp.where(hit, items, 0), axis=0, keepdims=True))
        own_kinds.append(jnp.sum(jnp.where(hit, kinds, 0), axis=0, keepdims=True))
        length = jnp.sum(jnp.where(hit, lens, 0), axis=0, keepdims=True)
        own_valid.append(jnp.where(iota((1, span), 1) < length, 1.0, 0.0))
    e_items = jnp.concatenate(own_items, axis=1)
    e_kinds = jnp.concatenate(own_kinds, axis=1)
    e_valid = jnp.concatenate(own_valid, axis=1)
    e_owner, _ = owner_and_row(e_items, e_kinds, row_counts)
    bucket = e_kinds * devices + e_owner
    member = onehot(iota((4 * devices, toks), 0) == bucket)
    before = onehot(iota((toks, toks), 0) < iota((toks, toks), 1))
    counts = dot(member, before)
    rank = jnp.sum(counts * member.astype(F32), axis=0, keepdims=True)
    slot = e_owner.astype(F32) * capacity + rank
    info = jnp.concatenate([slot, e_kinds.astype(F32), e_valid, jnp.zeros((5, toks), F32)], axis=0)
    info_ref[...] = info
    infot_ref[...] = jnp.transpose(
        jnp.concatenate([info, jnp.zeros((120, toks), F32)], axis=0), (1, 0)
    )
    owner, row = owner_and_row(items, kinds, row_counts)
    fields = jnp.concatenate(
        [
            jnp.where(owner == me, kinds, 4).astype(F32).astype(BF16),
            (row >> 7).astype(F32).astype(BF16),
            (row & 127).astype(F32).astype(BF16),
        ],
        axis=1,
    )
    moves = onehot(target == iota((seqs, seqs), 1))
    moved = dot(moves, fields, TN)
    m_kind = moved[:, :span]
    m_row = moved[:, span : 2 * span] * 128.0 + moved[:, 2 * span : 3 * span]
    hits = jnp.concatenate([onehot(m_kind == float(which)) for which in range(4)], axis=0)
    earlier = before[:span, :span]
    ahead = dot(hits, earlier)
    totals = jnp.sum(hits.astype(F32), axis=1, keepdims=True)
    si, sj = iota((seqs, seqs), 0), iota((seqs, seqs), 1)
    sibling = (floor_div(si, seq_count) == floor_div(sj, seq_count)) & (sj < si)
    code = jnp.full((seqs, span), -1.0, F32)
    for which in range(4):
        lo, hi = which * seqs, (which + 1) * seqs
        total = jnp.broadcast_to(totals[lo:hi], (seqs, 128)).astype(BF16)
        shift = dot(onehot(sibling), total)[:, 0:1]
        code = jnp.where(
            m_kind == float(which), ahead[lo:hi] + shift + float(which * capacity), code
        )
    asked = jnp.zeros((seqs, 128), F32)
    lane = iota((seqs, 128), 1)
    for tk in range(4 * capacity):
        value = jnp.sum(jnp.where(code == float(tk), m_row, 0.0), axis=1, keepdims=True)
        asked = jnp.where(lane == tk, value, asked)
    asked_high = jnp.floor(asked * (1.0 / 128.0))
    asked_low = asked - asked_high * 128.0
    spread = onehot(
        floor_div(iota((slots, seqs), 0), capacity) == floor_div(iota((slots, seqs), 1), seq_count)
    )
    full = dot(spread, asked_high.astype(BF16)) * 128.0 + dot(spread, asked_low.astype(BF16))
    place = iota((slots, 128), 0)
    place = place - floor_div(place, capacity) * capacity
    wide = iota((slots, 128), 1)
    columns = jnp.zeros((slots, 128), F32)
    highs, lows = [], []
    for which in range(4):
        index = jnp.sum(
            jnp.where(wide == place + which * capacity, full, 0.0), axis=1, keepdims=True
        )
        high = jnp.floor(index * (1.0 / SPLIT))
        low = index - high * SPLIT
        highs.append(high)
        lows.append(low)
        columns = jnp.where(wide == which, high, columns)
        columns = jnp.where(wide == which + 4, low, columns)
    idxc_ref[...] = columns
    idxr_ref[...] = jnp.transpose(columns, (1, 0))
    for copy in copies:
        copy.wait()
    low_lane = iota((slots, SPLIT), 1)

    def pick(which):
        return onehot(low_lane == lows[which].astype(jnp.int32))

    narrow = []
    for which in range(2):
        width = widths[which]
        steps = row_counts[which] // SPLIT
        group = 256 // width
        while steps % group:
            group //= 2
        chosen = pick(which)
        block = iota((slots, group * width), 1) >> log2(width)
        total = jnp.zeros((slots, group * width), F32)
        for g in range(steps // group):
            stack = jnp.concatenate(
                [
                    held[which][:, (g * group + b) * SPLIT : (g * group + b + 1) * SPLIT]
                    for b in range(group)
                ],
                axis=0,
            )
            found = dot(chosen, stack, NT)
            total = jnp.where(
                block + g * group == highs[which].astype(jnp.int32), found, total
            )
        folded = total[:, :128]
        for b in range(1, group * width // 128):
            folded = folded + total[:, b * 128 : (b + 1) * 128]
        folded = folded + pltpu.roll(folded, 64, 1)
        narrow.append(folded)
    rows_scr[0] = jnp.where(iota((slots, 128), 1) < widths[0], narrow[0], narrow[1])
    for which in range(2, 4):
        width = widths[which]
        chosen = pick(which)
        total = jnp.zeros((slots, width), F32)
        for step in range(row_counts[which] // SPLIT):
            found = dot(chosen, held[which][step * SPLIT : (step + 1) * SPLIT, :])
            total = jnp.where(highs[which] == float(step), found, total)
        for b in range(width // 128):
            rows_scr[which - 1 + b] = total[:, b * 128 : (b + 1) * 128]

    def pack(device, carry):
        for j in range(4):
            pack_scr[device, j * capacity : (j + 1) * capacity, :] = rows_scr[
                j, pl.ds(device * capacity, capacity), :
            ]
        return carry

    lax.fori_loop(0, devices, pack, 0)
    send_ref[...] = pack_scr[...].astype(BF16)


def layer_kernel(
    devices, seq_count, span, capacity, widths, dp_count, half, seq_a, seq_b, pieces, *refs
):
    me_ref, got_ref, info_ref, infot_ref, cot_ref = refs[:5]
    refs = refs[5:]
    a_refs, refs = refs[:pieces], refs[pieces:]
    b_refs, refs = refs[:pieces], refs[pieces:]
    out_ref, back_ref, ga_ref, gb_ref = refs[:4]
    (
        wa, wb, slot_scr, pack_scr, cat_scr, norm_scr, act_scr, slope_scr, attn_scr, tilt_scr,
        att_scr, datt_scr, dproj_scr, gated_scr, og_scr, demb_scr, drow_scr, dact_scr,
    ) = refs[4:]
    dp = me_ref[1]
    width = out_ref.shape[2]
    slots = devices * capacity
    toks = seq_count * span
    rows_each = width // dp_count
    head_dim = width // HEADS
    scale = head_dim**-0.5
    for refs_in, held, seq in ((a_refs, wa, seq_a), (b_refs, wb, seq_b)):
        index = 0
        for ref in refs_in:
            for k in range(ref.shape[0]):
                chunk = dp ^ mask_of(index, seq)
                start = pl.multiple_of(chunk * rows_each, rows_each)
                held[pl.ds(start, rows_each), :] = ref[k]
                index += 1
    pack_scr[...] = got_ref[...].astype(F32)

    def unpack(device, carry):
        for j in range(4):
            slot_scr[j, pl.ds(device * capacity, capacity), :] = pack_scr[
                device, j * capacity : (j + 1) * capacity, :
            ]
        return carry

    lax.fori_loop(0, devices, unpack, 0)
    arrived = jnp.concatenate([slot_scr[j].astype(BF16) for j in range(4)], axis=1)

    def in_part(j):
        return wa[:, j * width : (j + 1) * width] if j < 3 else wb[:, :width]

    lane = iota((span, width), 1)
    kind_of_lane = jnp.zeros((span, width), jnp.int32)
    edge = 0
    for which in range(3):
        edge += widths[which]
        kind_of_lane = kind_of_lane + jnp.where(lane >= edge, 1, 0)
    blocks = span // 128

    def sequence(q, carry):
        base = pl.multiple_of(q * span, span)
        rows = pl.ds(base, span)
        slot = infot_ref[rows, 0:1].astype(jnp.int32)
        kind = infot_ref[rows, 1:2].astype(jnp.int32)
        valid = infot_ref[rows, 2:3]
        chosen = onehot(iota((span, slots), 1) == slot)
        cat = jnp.where(kind_of_lane == kind, dot(chosen, arrived), 0.0).astype(BF16)
        cat_scr[rows, :] = cat
        emb = dot(cat, wb[:, 2 * width : 3 * width]).astype(BF16).astype(F32)
        centred = emb - jnp.mean(emb, axis=1, keepdims=True)
        inv = lax.rsqrt(jnp.mean(centred * centred, axis=1, keepdims=True) + 1e-05)
        normed = centred * inv
        norm_scr[rows, :] = normed.astype(BF16)
        for j in range(4):
            mixed = dot(norm_scr[rows, :], in_part(j))
            sig = sigmoid(mixed)
            part = mixed * sig
            act_scr[j] = part.astype(BF16)
            slope_scr[j] = sig + part * (1.0 - sig)
        for head in range(HEADS):
            cols = slice(head * head_dim, (head + 1) * head_dim)
            for rb in range(blocks):
                keys = (rb + 1) * 128
                here = slice(rb * 128, keys)
                scores = dot(act_scr[2, here, cols], act_scr[3, :keys, cols], NT) * scale
                key_pos = iota((128, keys), 1)
                keep = (key_pos <= iota((128, keys), 0) + rb * 128) & (
                    key_pos < carry_len(q, info_ref, span)
                )
                sig = sigmoid(scores)
                attn = scores * sig
                attn_scr[head, here, :keys] = jnp.where(keep, attn, 0.0).astype(BF16)
                tilt_scr[head, here, :keys] = jnp.where(
                    keep, (sig + attn * (1.0 - sig)) * scale, 0.0
                )
                att_scr[here, cols] = dot(
                    attn_scr[head, here, :keys], act_scr[1, :keys, cols]
                )
        attended = att_scr[...]
        att_c = attended - jnp.mean(attended, axis=1, keepdims=True)
        att_inv = lax.rsqrt(jnp.mean(att_c * att_c, axis=1, keepdims=True) + 1e-05)
        att_n = att_c * att_inv
        gate = act_scr[0].astype(F32)
        gated = (att_n * gate).astype(BF16)
        gated_scr[rows, :] = gated
        out_w = wb[:, width : 2 * width]
        out_ref[q] = (emb + dot(gated, out_w)).astype(BF16)
        og = jnp.where(valid > 0.5, cot_ref[q].astype(F32), 0.0).astype(BF16)
        og_scr[rows, :] = og
        d_gated = dot(og, out_w, NT).astype(BF16).astype(F32)
        d_gate = (d_gated * att_n).astype(BF16).astype(F32)
        dproj_scr[rows, :width] = (d_gate * slope_scr[0]).astype(BF16)
        d_n = d_gated * gate
        d_att = att_inv * (
            d_n
            - jnp.mean(d_n, axis=1, keepdims=True)
            - att_n * jnp.mean(d_n * att_n, axis=1, keepdims=True)
        )
        datt_scr[...] = d_att.astype(BF16)
        for head in range(HEADS):
            cols = slice(head * head_dim, (head + 1) * head_dim)
            for rb in range(blocks):
                keys = (rb + 1) * 128
                here = slice(rb * 128, keys)
                d_attn = dot(datt_scr[here, cols], act_scr[1, :keys, cols], NT)
                d_attn = d_attn.astype(BF16).astype(F32)
                tilt = (d_attn * tilt_scr[head, here, :keys]).astype(BF16)
                dact_scr[head, here, :keys] = tilt
                d_query = dot(tilt, act_scr[3, :keys, cols]).astype(BF16).astype(F32)
                low = 2 * width + head * head_dim
                dproj_scr[pl.ds(base + rb * 128, 128), low : low + head_dim] = (
                    d_query * slope_scr[2, here, cols]
                ).astype(BF16)
            for kb in range(blocks):
                here = slice(kb * 128, (kb + 1) * 128)
                rest = slice(kb * 128, span)
                d_value = dot(attn_scr[head, rest, here], datt_scr[rest, cols], TN)
                d_key = dot(dact_scr[head, rest, here], act_scr[2, rest, cols], TN)
                low = width + head * head_dim
                dproj_scr[pl.ds(base + kb * 128, 128), low : low + head_dim] = (
                    d_value.astype(BF16).astype(F32) * slope_scr[1, here, cols]
                ).astype(BF16)
                low = 3 * width + head * head_dim
                dproj_scr[pl.ds(base + kb * 128, 128), low : low + head_dim] = (
                    d_key.astype(BF16).astype(F32) * slope_scr[3, here, cols]
                ).astype(BF16)
        d_normed = jnp.zeros((span, width), F32)
        for j in range(4):
            d_normed = d_normed + dot(
                dproj_scr[rows, j * width : (j + 1) * width], in_part(j), NT
            )
        d_normed = d_normed.astype(BF16).astype(F32)
        d_emb = inv * (
            d_normed
            - jnp.mean(d_normed, axis=1, keepdims=True)
            - normed * jnp.mean(d_normed * normed, axis=1, keepdims=True)
        )
        d_emb = (d_emb + og.astype(F32)).astype(BF16)
        demb_scr[rows, :] = d_emb
        d_rows = dot(d_emb, wb[:, 2 * width : 3 * width], NT)
        drow_scr[rows, :] = jnp.where(kind_of_lane == kind, d_rows, 0.0).astype(BF16)
        return carry

    lax.fori_loop(0, seq_count, sequence, 0)
    chosen = onehot(iota((slots, toks), 0) == info_ref[0:1, :].astype(jnp.int32))
    outgoing = dot(chosen, drow_scr[...])
    for j in range(4):
        slot_scr[j] = outgoing[:, j * 128 : (j + 1) * 128]

    def pack(device, carry):
        for j in range(4):
            pack_scr[device, j * capacity : (j + 1) * capacity, :] = slot_scr[
                j, pl.ds(device * capacity, capacity), :
            ]
        return carry

    lax.fori_loop(0, devices, pack, 0)
    back_ref[...] = pack_scr[...].astype(BF16)

    def emit(grad, target, seq, low):
        grad = grad.astype(BF16)
        for chunk in range(dp_count):
            index = place_of(dp ^ chunk, seq)
            target[index, :, low : low + width] = grad[
                chunk * rows_each : (chunk + 1) * rows_each, :
            ]

    for j in range(4):
        grad = dot(norm_scr[...], dproj_scr[:, j * width : (j + 1) * width], TN)
        if j < 3:
            emit(grad, ga_ref, seq_a, j * width)
        else:
            emit(grad, gb_ref, seq_b, 0)
    emit(dot(gated_scr[...], og_scr[...], TN), gb_ref, seq_b, width)
    emit(dot(cat_scr[...], demb_scr[...], TN), gb_ref, seq_b, 2 * width)


def carry_len(q, info_ref, span):
    flags = info_ref[2:3, pl.ds(pl.multiple_of(q * span, 128), span)]
    return jnp.sum(flags, axis=1, keepdims=True).astype(jnp.int32)


def scatter_kernel(devices, capacity, row_counts, widths, *refs):
    got_ref, idxc_ref, idxr_ref = refs[:3]
    outs = refs[3:7]
    held = refs[7:11]
    slot_scr, pack_scr, sems = refs[11:]
    slots = devices * capacity
    pack_scr[...] = got_ref[...].astype(F32)

    def unpack(device, carry):
        for j in range(4):
            slot_scr[j, pl.ds(device * capacity, capacity), :] = pack_scr[
                device, j * capacity : (j + 1) * capacity, :
            ]
        return carry

    lax.fori_loop(0, devices, unpack, 0)
    copies = [pltpu.make_async_copy(held[i], outs[i], sems.at[i]) for i in range(4)]
    first = slot_scr[0]
    rolled = pltpu.roll(first, 64, 1)
    left = iota((slots, 128), 1) < widths[0]
    pairs = [jnp.where(left, first, rolled), jnp.where(left, rolled, first)]
    for which in range(2):
        width = widths[which]
        steps = row_counts[which] // SPLIT
        group = 256 // width
        while steps % group:
            group //= 2
        span = group * width
        high = idxc_ref[:, which : which + 1].astype(jnp.int32)
        low = idxc_ref[:, 4 + which : 5 + which].astype(jnp.int32)
        chosen = onehot(iota((slots, SPLIT), 1) == low)
        wide = jnp.concatenate([pairs[which]] * (span // 128), axis=1)
        block = iota((slots, span), 1) >> log2(width)
        for g in range(steps // group):
            part = jnp.where(block + g * group == high, wide, 0.0).astype(BF16)
            found = dot(part, chosen, TN).astype(BF16)
            for b in range(group):
                at = (g * group + b) * SPLIT
                held[which][:, at : at + SPLIT] = found[b * width : (b + 1) * width, :]
        copies[which].start()
    for which in range(2, 4):
        width = widths[which]
        steps = row_counts[which] // SPLIT
        group = 256 // width
        while steps % group:
            group //= 2
        high = idxc_ref[:, which : which + 1].astype(jnp.int32)
        low = idxr_ref[4 + which : 5 + which, :].astype(jnp.int32)
        chosen = onehot(iota((SPLIT, slots), 0) == low)
        wide = jnp.concatenate(
            [slot_scr[which - 1 + b] for b in range(width // 128)], axis=1
        )
        for g in range(steps // group):
            part = jnp.concatenate(
                [jnp.where(high == g * group + b, wide, 0.0).astype(BF16) for b in range(group)],
                axis=1,
            )
            found = dot(chosen, part).astype(BF16)
            for b in range(group):
                at = (g * group + b) * SPLIT
                held[which][at : at + SPLIT, :] = found[:, b * width : (b + 1) * width]
        copies[which].start()
    for copy in copies:
        copy.wait()


def split_kernel(planes, me_ref, ka_ref, ra_ref, kb_ref, rb_ref, *refs):
    outs, scr = refs[:planes], refs[planes]
    half = ka_ref.shape[1]
    scr[:, :half] = (ka_ref[...].astype(F32) + ra_ref[...].astype(F32)).astype(BF16)
    scr[:, half:] = (kb_ref[...].astype(F32) + rb_ref[...].astype(F32)).astype(BF16)
    size = outs[0].shape[1]
    for m in range(planes):
        at = pl.multiple_of((me_ref[2] ^ m) * size, 128)
        outs[m][...] = scr[:, pl.ds(at, size)]


def sum_kernel(*refs):
    total = refs[0][...].astype(F32)
    for ref in refs[1:-1]:
        total = total + ref[...].astype(F32)
    refs[-1][...] = total.astype(BF16)


def join_kernel(planes, width, me_ref, *refs):
    parts = refs[:planes]
    proj_ref, in_ref, out_ref, scr = refs[planes:]
    size = parts[0].shape[1]
    for m in range(planes):
        at = pl.multiple_of((me_ref[2] ^ m) * size, 128)
        scr[:, pl.ds(at, size)] = parts[m][...].astype(F32)
    in_ref[...] = scr[:, : 4 * width]
    out_ref[...] = scr[:, 4 * width : 5 * width]
    proj_ref[...] = scr[:, 5 * width :]


def exchange(value, axis, mask):
    count = lax.axis_size(axis)
    return lax.ppermute(value, axis, [(i, i ^ mask) for i in range(count)])


def params():
    return pltpu.CompilerParams(vmem_limit_bytes=60 * 1024 * 1024)


def shards(
    item_ids, table_ids, lengths, assignment, table_a, table_b, table_c, table_d,
    proj_weight, in_weight, out_weight, cotangent,
):
    tables = (table_a, table_b, table_c, table_d)
    dp_count = lax.axis_size("dp")
    planes = lax.axis_size("table")
    devices = dp_count * planes
    seq_count, span = item_ids.shape
    toks = seq_count * span
    width = cotangent.shape[2]
    capacity = max(2, toks // (2 * devices))
    slots = devices * capacity
    row_counts = tuple(piece.shape[0] for piece in tables)
    widths = tuple(piece.shape[1] for piece in tables)
    rows_each = width // dp_count
    dp_bits = log2(dp_count)
    dp = lax.axis_index("dp")
    plane = lax.axis_index("table")
    me = jnp.stack([dp * planes + plane, dp, plane]).astype(jnp.int32)
    half = 3 * width
    far = list(range(1, dp_bits))
    seq_a = [0] + far
    seq_b = [0] + far[::-1]
    own_a = in_weight[:, :half][None]
    own_b = jnp.concatenate([in_weight[:, half:], out_weight, proj_weight], axis=1)[None]

    def gather(own, seq):
        held = own
        for bit in seq[:0:-1]:
            held = jnp.concatenate([held, exchange(held, "dp", 1 << bit)], axis=0)
        return held, exchange(held, "dp", 1 << seq[0])

    pad = jnp.zeros((seq_count, 126), jnp.int32)
    packed = jnp.concatenate(
        [item_ids, table_ids, lengths[:, None], assignment[:, None], pad], axis=1
    )
    near = lax.all_gather(packed, "dp", axis=0, tiled=True)
    ids = [near] + [exchange(near, "table", m) for m in range(1, planes)]
    wa = gather(own_a, seq_a)
    wb = gather(own_b, seq_b)
    send, idxc, idxr, info, infot = pl.pallas_call(
        functools.partial(
            plan_kernel, planes, devices, seq_count, span, capacity, row_counts, widths
        ),
        out_shape=(
            jax.ShapeDtypeStruct((devices, 4 * capacity, 128), BF16),
            jax.ShapeDtypeStruct((slots, 128), F32),
            jax.ShapeDtypeStruct((128, slots), F32),
            jax.ShapeDtypeStruct((8, toks), F32),
            jax.ShapeDtypeStruct((toks, 128), F32),
        ),
        in_specs=[SM] + [VM] * planes + [HB] * 4,
        out_specs=(VM,) * 5,
        scratch_shapes=[
            pltpu.VMEM((widths[0], row_counts[0]), BF16),
            pltpu.VMEM((widths[1], row_counts[1]), BF16),
            pltpu.VMEM((row_counts[2], widths[2]), BF16),
            pltpu.VMEM((row_counts[3], widths[3]), BF16),
            pltpu.VMEM((4, slots, 128), F32),
            pltpu.VMEM((devices, 4 * capacity, 128), F32),
            pltpu.SemaphoreType.DMA((4,)),
        ],
        compiler_params=params(),
        name="plan",
    )(me, *ids, table_a.T, table_b.T, table_c, table_d)
    got = lax.all_to_all(send, ("dp", "table"), 0, 0, tiled=True)
    pieces = len(wa)
    output, back, grad_a, grad_b = pl.pallas_call(
        functools.partial(
            layer_kernel, devices, seq_count, span, capacity, widths, dp_count, half,
            seq_a, seq_b, pieces,
        ),
        out_shape=(
            jax.ShapeDtypeStruct((seq_count, span, width), BF16),
            jax.ShapeDtypeStruct((devices, 4 * capacity, 128), BF16),
            jax.ShapeDtypeStruct((dp_count, rows_each, half), BF16),
            jax.ShapeDtypeStruct((dp_count, rows_each, half), BF16),
        ),
        in_specs=[SM] + [VM] * (4 + 2 * pieces),
        out_specs=(VM,) * 4,
        scratch_shapes=[
            pltpu.VMEM((width, half), BF16),
            pltpu.VMEM((width, half), BF16),
            pltpu.VMEM((4, slots, 128), F32),
            pltpu.VMEM((devices, 4 * capacity, 128), F32),
            pltpu.VMEM((toks, width), BF16),
            pltpu.VMEM((toks, width), BF16),
            pltpu.VMEM((4, span, width), BF16),
            pltpu.VMEM((4, span, width), F32),
            pltpu.VMEM((HEADS, span, span), BF16),
            pltpu.VMEM((HEADS, span, span), F32),
            pltpu.VMEM((span, width), F32),
            pltpu.VMEM((span, width), BF16),
            pltpu.VMEM((toks, 4 * width), BF16),
            pltpu.VMEM((toks, width), BF16),
            pltpu.VMEM((toks, width), BF16),
            pltpu.VMEM((toks, width), BF16),
            pltpu.VMEM((toks, width), BF16),
            pltpu.VMEM((HEADS, span, span), BF16),
        ],
        compiler_params=params(),
        name="layer",
    )(me, got, info, infot, cotangent, *wa, *wb)

    def halve(held, seq):
        for place, bit in enumerate(seq):
            mid = held.shape[0] // 2
            taken = exchange(held[mid:], "dp", 1 << bit)
            if place == len(seq) - 1:
                return held[0], taken[0]
            held = (held[:mid].astype(F32) + taken.astype(F32)).astype(BF16)

    returned = lax.all_to_all(back, ("dp", "table"), 0, 0, tiled=True)
    kept_a, sent_a = halve(grad_a, seq_a)
    kept_b, sent_b = halve(grad_b, seq_b)
    size = 2 * half // planes
    parts = pl.pallas_call(
        functools.partial(split_kernel, planes),
        out_shape=(jax.ShapeDtypeStruct((rows_each, size), BF16),) * planes,
        in_specs=[SM] + [VM] * 4,
        out_specs=(VM,) * planes,
        scratch_shapes=[pltpu.VMEM((rows_each, 2 * half), BF16)],
        compiler_params=params(),
        name="split",
    )(me, kept_a, sent_a, kept_b, sent_b)
    terms = [parts[0]] + [exchange(parts[m], "table", m) for m in range(1, planes)]
    summed = pl.pallas_call(
        sum_kernel,
        out_shape=jax.ShapeDtypeStruct((rows_each, size), BF16),
        in_specs=[VM] * planes,
        out_specs=VM,
        compiler_params=params(),
        name="total",
    )(*terms)
    whole = [summed] + [exchange(summed, "table", m) for m in range(1, planes)]
    grad_proj, grad_in, grad_out = pl.pallas_call(
        functools.partial(join_kernel, planes, width),
        out_shape=(
            jax.ShapeDtypeStruct((rows_each, width), F32),
            jax.ShapeDtypeStruct((rows_each, 4 * width), F32),
            jax.ShapeDtypeStruct((rows_each, width), F32),
        ),
        in_specs=[SM] + [VM] * planes,
        out_specs=(VM,) * 3,
        scratch_shapes=[pltpu.VMEM((rows_each, 2 * half), F32)],
        compiler_params=params(),
        name="join",
    )(me, *whole)
    g_a, g_b, g_c, g_d = pl.pallas_call(
        functools.partial(scatter_kernel, devices, capacity, row_counts, widths),
        out_shape=(
            jax.ShapeDtypeStruct((widths[0], row_counts[0]), BF16),
            jax.ShapeDtypeStruct((widths[1], row_counts[1]), BF16),
            jax.ShapeDtypeStruct((row_counts[2], widths[2]), BF16),
            jax.ShapeDtypeStruct((row_counts[3], widths[3]), BF16),
        ),
        in_specs=[VM] * 3,
        out_specs=(HB,) * 4,
        scratch_shapes=[
            pltpu.VMEM((widths[0], row_counts[0]), BF16),
            pltpu.VMEM((widths[1], row_counts[1]), BF16),
            pltpu.VMEM((row_counts[2], widths[2]), BF16),
            pltpu.VMEM((row_counts[3], widths[3]), BF16),
            pltpu.VMEM((4, slots, 128), F32),
            pltpu.VMEM((devices, 4 * capacity, 128), F32),
            pltpu.SemaphoreType.DMA((4,)),
        ],
        compiler_params=params(),
        name="scatter",
    )(returned, idxc, idxr)
    return output, g_a.T, g_b.T, g_c, g_d, grad_proj, grad_in, grad_out


def solution(mesh):
    both = ("dp", "table")
    return jax.shard_map(
        shards,
        mesh=mesh,
        in_specs=(
            P(both, None), P(both, None), P(both), P(both),
            P(both, None), P(both, None), P(both, None), P(both, None),
            P("dp", None), P("dp", None), P("dp", None), P(both, None, None),
        ),
        out_specs=(
            P(both, None, None), P(both, None), P(both, None), P(both, None), P(both, None),
            P("dp", None), P("dp", None), P("dp", None),
        ),
        check_vma=False,
    )
```

```python
import functools

import jax
import jax.numpy as jnp
from jax import lax
from jax.experimental import pallas as pl
from jax.experimental.pallas import tpu as pltpu
from jax.sharding import PartitionSpec as P

HEADS = 4
SPLIT = 1024
F32 = jnp.float32
BF16 = jnp.bfloat16
NN = (((1,), (0,)), ((), ()))
NT = (((1,), (1,)), ((), ()))
TN = (((0,), (0,)), ((), ()))
VM = pl.BlockSpec(memory_space=pltpu.VMEM)
SM = pl.BlockSpec(memory_space=pltpu.SMEM)
HB = pl.BlockSpec(memory_space=pl.ANY)


def dot(left, right, dims=NN):
    return lax.dot_general(left, right, dims, preferred_element_type=F32)


def iota(shape, dim):
    return lax.broadcasted_iota(jnp.int32, shape, dim)


def onehot(flags):
    return jnp.where(flags, 1.0, 0.0).astype(BF16)


def floor_div(values, by):
    return jnp.floor((values.astype(F32) + 0.5) * (1.0 / by)).astype(jnp.int32)


def sigmoid(values):
    return 0.5 * jnp.tanh(0.5 * values) + 0.5


def log2(value):
    assert value & (value - 1) == 0
    return value.bit_length() - 1


def mask_of(index, seq):
    mask = 0
    for place, bit in enumerate(reversed(seq)):
        if (index >> place) & 1:
            mask |= 1 << bit
    return mask


def owner_and_row(items, kinds, row_counts):
    rows = jnp.zeros_like(items)
    inverse = jnp.zeros(items.shape, F32)
    for which in range(4):
        hit = kinds == which
        rows = jnp.where(hit, row_counts[which], rows)
        inverse = jnp.where(hit, 1.0 / row_counts[which], inverse)
    owner = jnp.floor(items.astype(F32) * inverse).astype(jnp.int32)
    rest = items - owner * rows
    low = rest < 0
    owner = jnp.where(low, owner - 1, owner)
    rest = jnp.where(low, rest + rows, rest)
    high = rest >= rows
    owner = jnp.where(high, owner + 1, owner)
    rest = jnp.where(high, rest - rows, rest)
    return owner, rest


def key_kernel(devices, row_counts, len_ref, to_ref, item_ref, kind_ref, out_ref):
    seq_count, span = item_ref.shape
    keys = item_ref[...]
    kinds = kind_ref[...]
    for which in range(3):
        edge = devices * sum(row_counts[: which + 1])
        keys = jnp.where(kinds == which + 1, item_ref[...] + edge, keys)
    lane = iota((1, 128), 1)
    rows = []
    for q in range(seq_count):
        for c in range(span // 128):
            rows.append(keys[q : q + 1, c * 128 : (c + 1) * 128])
        rows.append(jnp.where(lane == 0, len_ref[q], jnp.where(lane == 1, to_ref[q], 0)))
    block = jnp.concatenate(rows, axis=0)
    out_ref[...] = jnp.broadcast_to(block[None], out_ref.shape)


def plan_kernel(devices, seq_count, span, capacity, row_counts, widths, *refs):
    me_ref, ids_ref, refs = refs[0], refs[1], refs[2:]
    table_refs, refs = refs[:4], refs[4:]
    send_ref, idxc_ref, idxr_ref, info_ref, infot_ref = refs[:5]
    held = refs[5:9]
    rows_scr, pack_scr, sems = refs[9:]
    copies = [pltpu.make_async_copy(table_refs[i], held[i], sems.at[i]) for i in range(4)]
    for copy in copies:
        copy.start()
    me = me_ref[0]
    seqs = devices * seq_count
    slots = devices * capacity
    toks = seq_count * span
    lanes = ids_ref.shape[1] // seq_count
    chunks = span // 128
    keys = jnp.concatenate(
        [
            jnp.concatenate([ids_ref[:, q * lanes + c, :] for c in range(chunks)], axis=1)
            for q in range(seq_count)
        ],
        axis=0,
    )
    tail = jnp.concatenate(
        [ids_ref[:, q * lanes + chunks, :] for q in range(seq_count)], axis=0
    )
    kinds = jnp.zeros_like(keys)
    items = keys
    for which in range(3):
        edge = devices * sum(row_counts[: which + 1])
        kinds = kinds + jnp.where(keys >= edge, 1, 0)
        items = jnp.where(keys >= edge, keys - edge, items)
    lens = tail[:, 0:1]
    target = tail[:, 1:2]
    own_items, own_kinds, own_valid = [], [], []
    for q in range(seq_count):
        hit = target == me * seq_count + q
        own_items.append(jnp.sum(jnp.where(hit, items, 0), axis=0, keepdims=True))
        own_kinds.append(jnp.sum(jnp.where(hit, kinds, 0), axis=0, keepdims=True))
        length = jnp.sum(jnp.where(hit, lens, 0), axis=0, keepdims=True)
        own_valid.append(jnp.where(iota((1, span), 1) < length, 1.0, 0.0))
    e_items = jnp.concatenate(own_items, axis=1)
    e_kinds = jnp.concatenate(own_kinds, axis=1)
    e_valid = jnp.concatenate(own_valid, axis=1)
    e_owner, _ = owner_and_row(e_items, e_kinds, row_counts)
    bucket = e_kinds * devices + e_owner
    member = onehot(iota((4 * devices, toks), 0) == bucket)
    before = onehot(iota((toks, toks), 0) < iota((toks, toks), 1))
    counts = dot(member, before)
    rank = jnp.sum(counts * member.astype(F32), axis=0, keepdims=True)
    slot = e_owner.astype(F32) * capacity + rank
    info = jnp.concatenate([slot, e_kinds.astype(F32), e_valid, jnp.zeros((5, toks), F32)], axis=0)
    info_ref[...] = info
    infot_ref[...] = jnp.transpose(
        jnp.concatenate([info, jnp.zeros((120, toks), F32)], axis=0), (1, 0)
    )
    owner, row = owner_and_row(items, kinds, row_counts)
    fields = jnp.concatenate(
        [
            jnp.where(owner == me, kinds, 4).astype(F32).astype(BF16),
            (row >> 7).astype(F32).astype(BF16),
            (row & 127).astype(F32).astype(BF16),
        ],
        axis=1,
    )
    moves = onehot(target == iota((seqs, seqs), 1))
    moved = dot(moves, fields, TN)
    m_kind = moved[:, :span]
    m_row = moved[:, span : 2 * span] * 128.0 + moved[:, 2 * span : 3 * span]
    hits = jnp.concatenate([onehot(m_kind == float(which)) for which in range(4)], axis=0)
    earlier = before[:span, :span]
    ahead = dot(hits, earlier)
    totals = jnp.sum(hits.astype(F32), axis=1, keepdims=True)
    si, sj = iota((seqs, seqs), 0), iota((seqs, seqs), 1)
    sibling = (floor_div(si, seq_count) == floor_div(sj, seq_count)) & (sj < si)
    code = jnp.full((seqs, span), -1.0, F32)
    for which in range(4):
        lo, hi = which * seqs, (which + 1) * seqs
        total = jnp.broadcast_to(totals[lo:hi], (seqs, 128)).astype(BF16)
        shift = dot(onehot(sibling), total)[:, 0:1]
        code = jnp.where(
            m_kind == float(which), ahead[lo:hi] + shift + float(which * capacity), code
        )
    asked = jnp.zeros((seqs, 128), F32)
    lane = iota((seqs, 128), 1)
    for tk in range(4 * capacity):
        value = jnp.sum(jnp.where(code == float(tk), m_row, 0.0), axis=1, keepdims=True)
        asked = jnp.where(lane == tk, value, asked)
    asked_high = jnp.floor(asked * (1.0 / 128.0))
    asked_low = asked - asked_high * 128.0
    spread = onehot(
        floor_div(iota((slots, seqs), 0), capacity) == floor_div(iota((slots, seqs), 1), seq_count)
    )
    full = dot(spread, asked_high.astype(BF16)) * 128.0 + dot(spread, asked_low.astype(BF16))
    place = iota((slots, 128), 0)
    place = place - floor_div(place, capacity) * capacity
    wide = iota((slots, 128), 1)
    columns = jnp.zeros((slots, 128), F32)
    highs, lows = [], []
    for which in range(4):
        index = jnp.sum(
            jnp.where(wide == place + which * capacity, full, 0.0), axis=1, keepdims=True
        )
        high = jnp.floor(index * (1.0 / SPLIT))
        low = index - high * SPLIT
        highs.append(high)
        lows.append(low)
        columns = jnp.where(wide == which, high, columns)
        columns = jnp.where(wide == which + 4, low, columns)
    idxc_ref[...] = columns
    idxr_ref[...] = jnp.transpose(columns, (1, 0))
    for copy in copies:
        copy.wait()
    low_lane = iota((slots, SPLIT), 1)

    def pick(which):
        return onehot(low_lane == lows[which].astype(jnp.int32))

    narrow = []
    for which in range(2):
        width = widths[which]
        steps = row_counts[which] // SPLIT
        group = 256 // width
        while steps % group:
            group //= 2
        chosen = pick(which)
        block = iota((slots, group * width), 1) >> log2(width)
        total = jnp.zeros((slots, group * width), F32)
        for g in range(steps // group):
            stack = jnp.concatenate(
                [
                    held[which][:, (g * group + b) * SPLIT : (g * group + b + 1) * SPLIT]
                    for b in range(group)
                ],
                axis=0,
            )
            found = dot(chosen, stack, NT)
            total = jnp.where(
                block + g * group == highs[which].astype(jnp.int32), found, total
            )
        folded = total[:, :128]
        for b in range(1, group * width // 128):
            folded = folded + total[:, b * 128 : (b + 1) * 128]
        folded = folded + pltpu.roll(folded, 64, 1)
        narrow.append(folded)
    rows_scr[0] = jnp.where(iota((slots, 128), 1) < widths[0], narrow[0], narrow[1])
    for which in range(2, 4):
        width = widths[which]
        chosen = pick(which)
        total = jnp.zeros((slots, width), F32)
        for step in range(row_counts[which] // SPLIT):
            found = dot(chosen, held[which][step * SPLIT : (step + 1) * SPLIT, :])
            total = jnp.where(highs[which] == float(step), found, total)
        for b in range(width // 128):
            rows_scr[which - 1 + b] = total[:, b * 128 : (b + 1) * 128]

    def pack(device, carry):
        for j in range(4):
            pack_scr[device, j * capacity : (j + 1) * capacity, :] = rows_scr[
                j, pl.ds(device * capacity, capacity), :
            ]
        return carry

    lax.fori_loop(0, devices, pack, 0)
    send_ref[...] = pack_scr[...].astype(BF16)


def layer_kernel(
    devices, planes, seq_count, span, capacity, widths, dp_count, half, seq_a, seq_b, pieces, *refs
):
    me_ref, got_ref, info_ref, infot_ref, cot_ref = refs[:5]
    refs = refs[5:]
    a_refs, refs = refs[:pieces], refs[pieces:]
    b_refs, refs = refs[:pieces], refs[pieces:]
    out_ref, back_ref, ga_keep, ga_send, gb_keep, gb_send = refs[:6]
    (
        wa, wb, slot_scr, pack_scr, cat_scr, norm_scr, act_scr, slope_scr, attn_scr, tilt_scr,
        att_scr, datt_scr, dproj_scr, gated_scr, og_scr, demb_scr, drow_scr, dact_scr,
        grad_scr,
    ) = refs[6:]
    dp = me_ref[1]
    width = out_ref.shape[2]
    slots = devices * capacity
    toks = seq_count * span
    rows_each = width // dp_count
    head_dim = width // HEADS
    scale = head_dim**-0.5
    for refs_in, held, seq in ((a_refs, wa, seq_a), (b_refs, wb, seq_b)):
        index = 0
        for ref in refs_in:
            for k in range(ref.shape[0]):
                chunk = dp ^ mask_of(index, seq)
                start = pl.multiple_of(chunk * rows_each, rows_each)
                held[pl.ds(start, rows_each), :] = ref[k]
                index += 1
    pack_scr[...] = got_ref[...].astype(F32)

    def unpack(device, carry):
        for j in range(4):
            slot_scr[j, pl.ds(device * capacity, capacity), :] = pack_scr[
                device, j * capacity : (j + 1) * capacity, :
            ]
        return carry

    lax.fori_loop(0, devices, unpack, 0)
    arrived = jnp.concatenate([slot_scr[j].astype(BF16) for j in range(4)], axis=1)

    def in_part(j):
        return wa[:, j * width : (j + 1) * width] if j < 3 else wb[:, :width]

    lane = iota((span, width), 1)
    kind_of_lane = jnp.zeros((span, width), jnp.int32)
    edge = 0
    for which in range(3):
        edge += widths[which]
        kind_of_lane = kind_of_lane + jnp.where(lane >= edge, 1, 0)
    blocks = span // 128

    def sequence(q, carry):
        base = pl.multiple_of(q * span, span)
        rows = pl.ds(base, span)
        slot = infot_ref[rows, 0:1].astype(jnp.int32)
        kind = infot_ref[rows, 1:2].astype(jnp.int32)
        valid = infot_ref[rows, 2:3]
        chosen = onehot(iota((span, slots), 1) == slot)
        cat = jnp.where(kind_of_lane == kind, dot(chosen, arrived), 0.0).astype(BF16)
        cat_scr[rows, :] = cat
        emb = dot(cat, wb[:, 2 * width : 3 * width]).astype(BF16).astype(F32)
        centred = emb - jnp.mean(emb, axis=1, keepdims=True)
        inv = lax.rsqrt(jnp.mean(centred * centred, axis=1, keepdims=True) + 1e-05)
        normed = centred * inv
        norm_scr[rows, :] = normed.astype(BF16)
        for j in range(4):
            mixed = dot(norm_scr[rows, :], in_part(j))
            sig = sigmoid(mixed)
            part = mixed * sig
            act_scr[j] = part.astype(BF16)
            slope_scr[j] = sig + part * (1.0 - sig)
        for head in range(HEADS):
            cols = slice(head * head_dim, (head + 1) * head_dim)
            for rb in range(blocks):
                keys = (rb + 1) * 128
                here = slice(rb * 128, keys)
                scores = dot(act_scr[2, here, cols], act_scr[3, :keys, cols], NT) * scale
                key_pos = iota((128, keys), 1)
                keep = (key_pos <= iota((128, keys), 0) + rb * 128) & (
                    key_pos < carry_len(q, info_ref, span)
                )
                sig = sigmoid(scores)
                attn = scores * sig
                attn_scr[head, here, :keys] = jnp.where(keep, attn, 0.0).astype(BF16)
                tilt_scr[head, here, :keys] = jnp.where(
                    keep, (sig + attn * (1.0 - sig)) * scale, 0.0
                )
                att_scr[here, cols] = dot(
                    attn_scr[head, here, :keys], act_scr[1, :keys, cols]
                )
        attended = att_scr[...]
        att_c = attended - jnp.mean(attended, axis=1, keepdims=True)
        att_inv = lax.rsqrt(jnp.mean(att_c * att_c, axis=1, keepdims=True) + 1e-05)
        att_n = att_c * att_inv
        gate = act_scr[0].astype(F32)
        gated = (att_n * gate).astype(BF16)
        gated_scr[rows, :] = gated
        out_w = wb[:, width : 2 * width]
        out_ref[q] = (emb + dot(gated, out_w)).astype(BF16)
        og = jnp.where(valid > 0.5, cot_ref[q].astype(F32), 0.0).astype(BF16)
        og_scr[rows, :] = og
        d_gated = dot(og, out_w, NT).astype(BF16).astype(F32)
        d_gate = (d_gated * att_n).astype(BF16).astype(F32)
        dproj_scr[rows, :width] = (d_gate * slope_scr[0]).astype(BF16)
        d_n = d_gated * gate
        d_att = att_inv * (
            d_n
            - jnp.mean(d_n, axis=1, keepdims=True)
            - att_n * jnp.mean(d_n * att_n, axis=1, keepdims=True)
        )
        datt_scr[...] = d_att.astype(BF16)
        for head in range(HEADS):
            cols = slice(head * head_dim, (head + 1) * head_dim)
            for rb in range(blocks):
                keys = (rb + 1) * 128
                here = slice(rb * 128, keys)
                d_attn = dot(datt_scr[here, cols], act_scr[1, :keys, cols], NT)
                d_attn = d_attn.astype(BF16).astype(F32)
                tilt = (d_attn * tilt_scr[head, here, :keys]).astype(BF16)
                dact_scr[head, here, :keys] = tilt
                d_query = dot(tilt, act_scr[3, :keys, cols]).astype(BF16).astype(F32)
                low = 2 * width + head * head_dim
                dproj_scr[pl.ds(base + rb * 128, 128), low : low + head_dim] = (
                    d_query * slope_scr[2, here, cols]
                ).astype(BF16)
            for kb in range(blocks):
                here = slice(kb * 128, (kb + 1) * 128)
                rest = slice(kb * 128, span)
                d_value = dot(attn_scr[head, rest, here], datt_scr[rest, cols], TN)
                d_key = dot(dact_scr[head, rest, here], act_scr[2, rest, cols], TN)
                low = width + head * head_dim
                dproj_scr[pl.ds(base + kb * 128, 128), low : low + head_dim] = (
                    d_value.astype(BF16).astype(F32) * slope_scr[1, here, cols]
                ).astype(BF16)
                low = 3 * width + head * head_dim
                dproj_scr[pl.ds(base + kb * 128, 128), low : low + head_dim] = (
                    d_key.astype(BF16).astype(F32) * slope_scr[3, here, cols]
                ).astype(BF16)
        d_normed = jnp.zeros((span, width), F32)
        for j in range(4):
            d_normed = d_normed + dot(
                dproj_scr[rows, j * width : (j + 1) * width], in_part(j), NT
            )
        d_normed = d_normed.astype(BF16).astype(F32)
        d_emb = inv * (
            d_normed
            - jnp.mean(d_normed, axis=1, keepdims=True)
            - normed * jnp.mean(d_normed * normed, axis=1, keepdims=True)
        )
        d_emb = (d_emb + og.astype(F32)).astype(BF16)
        demb_scr[rows, :] = d_emb
        d_rows = dot(d_emb, wb[:, 2 * width : 3 * width], NT)
        drow_scr[rows, :] = jnp.where(kind_of_lane == kind, d_rows, 0.0).astype(BF16)
        return carry

    lax.fori_loop(0, seq_count, sequence, 0)
    chosen = onehot(iota((slots, toks), 0) == info_ref[0:1, :].astype(jnp.int32))
    outgoing = dot(chosen, drow_scr[...])
    for j in range(4):
        slot_scr[j] = outgoing[:, j * 128 : (j + 1) * 128]

    def pack(device, carry):
        for j in range(4):
            pack_scr[device, j * capacity : (j + 1) * capacity, :] = slot_scr[
                j, pl.ds(device * capacity, capacity), :
            ]
        return carry

    lax.fori_loop(0, devices, pack, 0)
    back_ref[...] = pack_scr[...].astype(BF16)

    def emit(grad, low):
        grad_scr[:, low : low + width] = grad.astype(BF16)

    for j in range(4):
        emit(dot(norm_scr[...], dproj_scr[:, j * width : (j + 1) * width], TN), j * width)
    emit(dot(gated_scr[...], og_scr[...], TN), 4 * width)
    emit(dot(cat_scr[...], demb_scr[...], TN), 5 * width)
    middle = dp_count // 2
    size = 2 * half // planes
    for part in range(planes):
        side, slot_at = divmod(part, planes // 2)
        seq = (seq_a, seq_b)[side]
        pair = ((ga_keep, ga_send), (gb_keep, gb_send))[side]
        lanes = pl.ds(pl.multiple_of((me_ref[2] ^ part) * size, 128), size)
        for index in range(dp_count):
            chunk = dp ^ mask_of(index, seq)
            rows = pl.ds(pl.multiple_of(chunk * rows_each, rows_each), rows_each)
            pair[index // middle][
                index % middle, :, slot_at * size : (slot_at + 1) * size
            ] = grad_scr[rows, lanes]


def carry_len(q, info_ref, span):
    flags = info_ref[2:3, pl.ds(pl.multiple_of(q * span, 128), span)]
    return jnp.sum(flags, axis=1, keepdims=True).astype(jnp.int32)


def scatter_kernel(devices, capacity, row_counts, widths, *refs):
    got_ref, idxc_ref, idxr_ref = refs[:3]
    outs = refs[3:7]
    held = refs[7:11]
    slot_scr, pack_scr, sems = refs[11:]
    slots = devices * capacity
    pack_scr[...] = got_ref[...].astype(F32)

    def unpack(device, carry):
        for j in range(4):
            slot_scr[j, pl.ds(device * capacity, capacity), :] = pack_scr[
                device, j * capacity : (j + 1) * capacity, :
            ]
        return carry

    lax.fori_loop(0, devices, unpack, 0)
    copies = [pltpu.make_async_copy(held[i], outs[i], sems.at[i]) for i in range(4)]
    first = slot_scr[0]
    rolled = pltpu.roll(first, 64, 1)
    left = iota((slots, 128), 1) < widths[0]
    pairs = [jnp.where(left, first, rolled), jnp.where(left, rolled, first)]
    for which in range(2):
        width = widths[which]
        steps = row_counts[which] // SPLIT
        group = 256 // width
        while steps % group:
            group //= 2
        span = group * width
        high = idxc_ref[:, which : which + 1].astype(jnp.int32)
        low = idxc_ref[:, 4 + which : 5 + which].astype(jnp.int32)
        chosen = onehot(iota((slots, SPLIT), 1) == low)
        wide = jnp.concatenate([pairs[which]] * (span // 128), axis=1)
        block = iota((slots, span), 1) >> log2(width)
        for g in range(steps // group):
            part = jnp.where(block + g * group == high, wide, 0.0).astype(BF16)
            found = dot(part, chosen, TN).astype(BF16)
            for b in range(group):
                at = (g * group + b) * SPLIT
                held[which][:, at : at + SPLIT] = found[b * width : (b + 1) * width, :]
        copies[which].start()
    for which in range(2, 4):
        width = widths[which]
        steps = row_counts[which] // SPLIT
        group = 256 // width
        while steps % group:
            group //= 2
        high = idxc_ref[:, which : which + 1].astype(jnp.int32)
        low = idxr_ref[4 + which : 5 + which, :].astype(jnp.int32)
        chosen = onehot(iota((SPLIT, slots), 0) == low)
        wide = jnp.concatenate(
            [slot_scr[which - 1 + b] for b in range(width // 128)], axis=1
        )
        for g in range(steps // group):
            part = jnp.concatenate(
                [jnp.where(high == g * group + b, wide, 0.0).astype(BF16) for b in range(group)],
                axis=1,
            )
            found = dot(chosen, part).astype(BF16)
            for b in range(group):
                at = (g * group + b) * SPLIT
                held[which][at : at + SPLIT, :] = found[:, b * width : (b + 1) * width]
        copies[which].start()
    for copy in copies:
        copy.wait()


def join_kernel(planes, width, me_ref, *refs):
    parts = refs[:planes]
    proj_ref, in_ref, out_ref, scr = refs[planes:]
    size = parts[0].shape[1]
    for m in range(planes):
        at = pl.multiple_of((me_ref[2] ^ m) * size, 128)
        scr[:, pl.ds(at, size)] = parts[m][...].astype(F32)
    in_ref[...] = scr[:, : 4 * width]
    out_ref[...] = scr[:, 4 * width : 5 * width]
    proj_ref[...] = scr[:, 5 * width :]


def exchange(value, axis, mask):
    count = lax.axis_size(axis)
    return lax.ppermute(value, axis, [(i, i ^ mask) for i in range(count)])


def params(mib):
    return pltpu.CompilerParams(vmem_limit_bytes=mib * 1024 * 1024)


def step(
    item_ids, table_ids, lengths, assignment, table_a, table_b, table_c, table_d,
    proj_weight, in_weight, out_weight, cotangent,
):
    tables = (table_a, table_b, table_c, table_d)
    dp_count = lax.axis_size("dp")
    planes = lax.axis_size("table")
    devices = dp_count * planes
    seq_count, span = item_ids.shape
    toks = seq_count * span
    width = cotangent.shape[2]
    capacity = max(2, toks // (2 * devices))
    slots = devices * capacity
    row_counts = tuple(piece.shape[0] for piece in tables)
    widths = tuple(piece.shape[1] for piece in tables)
    rows_each = width // dp_count
    dp_bits = log2(dp_count)
    dp = lax.axis_index("dp")
    plane = lax.axis_index("table")
    me = jnp.stack([dp * planes + plane, dp, plane]).astype(jnp.int32)
    half = 3 * width
    far = list(range(1, dp_bits))
    seq_a = [0] + far
    seq_b = [0] + far[::-1]
    lanes = span // 128 + 1
    packed = pl.pallas_call(
        functools.partial(key_kernel, devices, row_counts),
        out_shape=jax.ShapeDtypeStruct((devices, seq_count * lanes, 128), jnp.int32),
        in_specs=[SM, SM, VM, VM],
        out_specs=VM,
        compiler_params=params(60),
        name="key",
    )(lengths, assignment, item_ids, table_ids)
    packed, in_weight, out_weight, proj_weight = lax.optimization_barrier(
        (packed, in_weight, out_weight, proj_weight)
    )
    ids = lax.all_to_all(packed, ("dp", "table"), 0, 0, tiled=True)
    own_a = in_weight[:, :half][None]
    own_b = jnp.concatenate([in_weight[:, half:], out_weight, proj_weight], axis=1)[None]

    def gather(held, taken, seq):
        bits = seq[:0:-1]
        for place, bit in enumerate(bits):
            if place:
                taken = exchange(held, "dp", 1 << bit)
            held = jnp.concatenate([held, taken], axis=0)
        return held

    first_a = exchange(own_a, "dp", 1 << seq_a[-1])
    first_b = exchange(own_b, "dp", 1 << seq_b[-1])
    send, idxc, idxr, info, infot = pl.pallas_call(
        functools.partial(
            plan_kernel, devices, seq_count, span, capacity, row_counts, widths
        ),
        out_shape=(
            jax.ShapeDtypeStruct((devices, 4 * capacity, 128), BF16),
            jax.ShapeDtypeStruct((slots, 128), F32),
            jax.ShapeDtypeStruct((128, slots), F32),
            jax.ShapeDtypeStruct((8, toks), F32),
            jax.ShapeDtypeStruct((toks, 128), F32),
        ),
        in_specs=[SM, VM] + [HB] * 4,
        out_specs=(VM,) * 5,
        scratch_shapes=[
            pltpu.VMEM((widths[0], row_counts[0]), BF16),
            pltpu.VMEM((widths[1], row_counts[1]), BF16),
            pltpu.VMEM((row_counts[2], widths[2]), BF16),
            pltpu.VMEM((row_counts[3], widths[3]), BF16),
            pltpu.VMEM((4, slots, 128), F32),
            pltpu.VMEM((devices, 4 * capacity, 128), F32),
            pltpu.SemaphoreType.DMA((4,)),
        ],
        compiler_params=params(60),
        name="plan",
    )(me, ids, table_a.T, table_b.T, table_c, table_d)
    send, first_a, first_b = lax.optimization_barrier((send, first_a, first_b))
    near_a = gather(own_a, first_a, seq_a)
    near_b = gather(own_b, first_b, seq_b)
    got = lax.all_to_all(send, ("dp", "table"), 0, 0, tiled=True)
    wa = (near_a, exchange(near_a, "dp", 1 << seq_a[0]))
    wb = (near_b, exchange(near_b, "dp", 1 << seq_b[0]))
    pieces = len(wa)
    output, back, keep_a, send_a, keep_b, send_b = pl.pallas_call(
        functools.partial(
            layer_kernel, devices, planes, seq_count, span, capacity, widths, dp_count, half,
            seq_a, seq_b, pieces,
        ),
        out_shape=(
            jax.ShapeDtypeStruct((seq_count, span, width), BF16),
            jax.ShapeDtypeStruct((devices, 4 * capacity, 128), BF16),
        )
        + (jax.ShapeDtypeStruct((dp_count // 2, rows_each, half), BF16),) * 4,
        in_specs=[SM] + [VM] * (4 + 2 * pieces),
        out_specs=(VM,) * 6,
        scratch_shapes=[
            pltpu.VMEM((width, half), BF16),
            pltpu.VMEM((width, half), BF16),
            pltpu.VMEM((4, slots, 128), F32),
            pltpu.VMEM((devices, 4 * capacity, 128), F32),
            pltpu.VMEM((toks, width), BF16),
            pltpu.VMEM((toks, width), BF16),
            pltpu.VMEM((4, span, width), BF16),
            pltpu.VMEM((4, span, width), F32),
            pltpu.VMEM((HEADS, span, span), BF16),
            pltpu.VMEM((HEADS, span, span), F32),
            pltpu.VMEM((span, width), F32),
            pltpu.VMEM((span, width), BF16),
            pltpu.VMEM((toks, 4 * width), BF16),
            pltpu.VMEM((toks, width), BF16),
            pltpu.VMEM((toks, width), BF16),
            pltpu.VMEM((toks, width), BF16),
            pltpu.VMEM((toks, width), BF16),
            pltpu.VMEM((HEADS, span, span), BF16),
            pltpu.VMEM((width, 2 * half), BF16),
        ],
        compiler_params=params(48),
        name="layer",
    )(me, got, info, infot, cotangent, *wa, *wb)

    def halve(keep, send, seq):
        for place, bit in enumerate(seq):
            taken = exchange(send, "dp", 1 << bit)
            if place == len(seq) - 1:
                return keep[0], taken[0]
            mid = keep.shape[0] // 2
            send = (keep[mid:].astype(F32) + taken[mid:].astype(F32)).astype(BF16)
            keep = (keep[:mid].astype(F32) + taken[:mid].astype(F32)).astype(BF16)

    returned = lax.all_to_all(back, ("dp", "table"), 0, 0, tiled=True)
    kept_a, sent_a = halve(keep_a, send_a, seq_a)
    kept_b, sent_b = halve(keep_b, send_b, seq_b)
    size = 2 * half // planes
    parts = []
    for kept, sent in ((kept_a, sent_a), (kept_b, sent_b)):
        for low in range(0, half, size):
            cut = slice(low, low + size)
            parts.append((kept[:, cut].astype(F32) + sent[:, cut].astype(F32)).astype(BF16))
    total = parts[0].astype(F32)
    for m in range(1, planes):
        total = total + exchange(parts[m], "table", m).astype(F32)
    summed = total.astype(BF16)
    whole = [summed] + [exchange(summed, "table", m) for m in range(1, planes)]
    grad_proj, grad_in, grad_out = pl.pallas_call(
        functools.partial(join_kernel, planes, width),
        out_shape=(
            jax.ShapeDtypeStruct((rows_each, width), F32),
            jax.ShapeDtypeStruct((rows_each, 4 * width), F32),
            jax.ShapeDtypeStruct((rows_each, width), F32),
        ),
        in_specs=[SM] + [VM] * planes,
        out_specs=(VM,) * 3,
        scratch_shapes=[pltpu.VMEM((rows_each, 2 * half), F32)],
        compiler_params=params(6),
        name="join",
    )(me, *whole)
    g_a, g_b, g_c, g_d = pl.pallas_call(
        functools.partial(scatter_kernel, devices, capacity, row_counts, widths),
        out_shape=(
            jax.ShapeDtypeStruct((widths[0], row_counts[0]), BF16),
            jax.ShapeDtypeStruct((widths[1], row_counts[1]), BF16),
            jax.ShapeDtypeStruct((row_counts[2], widths[2]), BF16),
            jax.ShapeDtypeStruct((row_counts[3], widths[3]), BF16),
        ),
        in_specs=[VM] * 3,
        out_specs=(HB,) * 4,
        scratch_shapes=[
            pltpu.VMEM((widths[0], row_counts[0]), BF16),
            pltpu.VMEM((widths[1], row_counts[1]), BF16),
            pltpu.VMEM((row_counts[2], widths[2]), BF16),
            pltpu.VMEM((row_counts[3], widths[3]), BF16),
            pltpu.VMEM((4, slots, 128), F32),
            pltpu.VMEM((devices, 4 * capacity, 128), F32),
            pltpu.SemaphoreType.DMA((4,)),
        ],
        compiler_params=params(26),
        name="scatter",
    )(returned, idxc, idxr)
    return output, g_a.T, g_b.T, g_c, g_d, grad_proj, grad_in, grad_out


def solution(mesh):
    both = ("dp", "table")
    return jax.shard_map(
        step,
        mesh=mesh,
        in_specs=(
            P(both, None), P(both, None), P(both), P(both),
            P(both, None), P(both, None), P(both, None), P(both, None),
            P("dp", None), P("dp", None), P("dp", None), P(both, None, None),
        ),
        out_specs=(
            P(both, None, None), P(both, None), P(both, None), P(both, None), P(both, None),
            P("dp", None), P("dp", None), P("dp", None),
        ),
        check_vma=False,
    )
```

```python
import functools

import jax
import jax.numpy as jnp
from jax import lax
from jax.experimental import pallas as pl
from jax.experimental.pallas import tpu as pltpu
from jax.sharding import PartitionSpec as P

HEADS = 4
SPLIT = 1024
F32 = jnp.float32
BF16 = jnp.bfloat16
NN = (((1,), (0,)), ((), ()))
NT = (((1,), (1,)), ((), ()))
TN = (((0,), (0,)), ((), ()))
VM = pl.BlockSpec(memory_space=pltpu.VMEM)
SM = pl.BlockSpec(memory_space=pltpu.SMEM)
HB = pl.BlockSpec(memory_space=pl.ANY)


def dot(left, right, dims=NN):
    return lax.dot_general(left, right, dims, preferred_element_type=F32)


def iota(shape, dim):
    return lax.broadcasted_iota(jnp.int32, shape, dim)


def onehot(flags):
    return jnp.where(flags, 1.0, 0.0).astype(BF16)


def floor_div(values, by):
    return jnp.floor((values.astype(F32) + 0.5) * (1.0 / by)).astype(jnp.int32)


def log2(value):
    assert value & (value - 1) == 0
    return value.bit_length() - 1


def mask_of(index, seq):
    mask = 0
    for place, bit in enumerate(reversed(seq)):
        if (index >> place) & 1:
            mask |= 1 << bit
    return mask


def owner_and_row(items, kinds, row_counts):
    rows = jnp.zeros_like(items)
    inverse = jnp.zeros(items.shape, F32)
    for which in range(4):
        hit = kinds == which
        rows = jnp.where(hit, row_counts[which], rows)
        inverse = jnp.where(hit, 1.0 / row_counts[which], inverse)
    owner = jnp.floor(items.astype(F32) * inverse).astype(jnp.int32)
    rest = items - owner * rows
    low = rest < 0
    owner = jnp.where(low, owner - 1, owner)
    rest = jnp.where(low, rest + rows, rest)
    high = rest >= rows
    owner = jnp.where(high, owner + 1, owner)
    rest = jnp.where(high, rest - rows, rest)
    return owner, rest


def key_kernel(devices, row_counts, len_ref, to_ref, item_ref, kind_ref, out_ref):
    seq_count, span = item_ref.shape
    keys = item_ref[...]
    kinds = kind_ref[...]
    for which in range(3):
        edge = devices * sum(row_counts[: which + 1])
        keys = jnp.where(kinds == which + 1, item_ref[...] + edge, keys)
    lane = iota((1, 128), 1)
    rows = []
    for q in range(seq_count):
        for c in range(span // 128):
            rows.append(keys[q : q + 1, c * 128 : (c + 1) * 128])
        rows.append(jnp.where(lane == 0, len_ref[q], jnp.where(lane == 1, to_ref[q], 0)))
    block = jnp.concatenate(rows, axis=0)
    out_ref[...] = jnp.broadcast_to(block[None], out_ref.shape)


def read_ids(ids_ref, devices, seq_count, span, row_counts):
    lanes = ids_ref.shape[1] // seq_count
    chunks = span // 128
    keys = jnp.concatenate(
        [
            jnp.concatenate([ids_ref[:, q * lanes + c, :] for c in range(chunks)], axis=1)
            for q in range(seq_count)
        ],
        axis=0,
    )
    tail = jnp.concatenate(
        [ids_ref[:, q * lanes + chunks, :] for q in range(seq_count)], axis=0
    )
    kinds = jnp.zeros_like(keys)
    items = keys
    for which in range(3):
        edge = devices * sum(row_counts[: which + 1])
        kinds = kinds + jnp.where(keys >= edge, 1, 0)
        items = jnp.where(keys >= edge, keys - edge, items)
    lens = tail[:, 0:1]
    target = tail[:, 1:2]
    return items, kinds, lens, target


def own_kernel(devices, seq_count, span, capacity, row_counts, *refs):
    me_ref, ids_ref, idxc_ref, idxr_ref, info_ref, infot_ref = refs
    me = me_ref[0]
    toks = seq_count * span
    idxr_ref[...] = jnp.transpose(idxc_ref[...], (1, 0))
    items, kinds, lens, target = read_ids(ids_ref, devices, seq_count, span, row_counts)
    own_items, own_kinds, own_valid = [], [], []
    for q in range(seq_count):
        hit = target == me * seq_count + q
        own_items.append(jnp.sum(jnp.where(hit, items, 0), axis=0, keepdims=True))
        own_kinds.append(jnp.sum(jnp.where(hit, kinds, 0), axis=0, keepdims=True))
        length = jnp.sum(jnp.where(hit, lens, 0), axis=0, keepdims=True)
        own_valid.append(jnp.where(iota((1, span), 1) < length, 1.0, 0.0))
    e_items = jnp.concatenate(own_items, axis=1)
    e_kinds = jnp.concatenate(own_kinds, axis=1)
    e_valid = jnp.concatenate(own_valid, axis=1)
    e_owner, _ = owner_and_row(e_items, e_kinds, row_counts)
    bucket = e_kinds * devices + e_owner
    member = onehot(iota((4 * devices, toks), 0) == bucket)
    before = onehot(iota((toks, toks), 0) < iota((toks, toks), 1))
    counts = dot(member, before)
    rank = jnp.sum(counts * member.astype(F32), axis=0, keepdims=True)
    slot = e_owner.astype(F32) * capacity + rank
    info = jnp.concatenate([slot, e_kinds.astype(F32), e_valid, jnp.zeros((5, toks), F32)], axis=0)
    info_ref[...] = info
    infot_ref[...] = jnp.transpose(
        jnp.concatenate([info, jnp.zeros((120, toks), F32)], axis=0), (1, 0)
    )


def plan_kernel(devices, seq_count, span, capacity, row_counts, widths, *refs):
    me_ref, ids_ref, refs = refs[0], refs[1], refs[2:]
    table_refs, refs = refs[:4], refs[4:]
    send_ref, idxc_ref = refs[:2]
    held = refs[2:6]
    rows_scr, pack_scr, sems = refs[6:]
    copies = [pltpu.make_async_copy(table_refs[i], held[i], sems.at[i]) for i in range(4)]
    for copy in copies:
        copy.start()
    me = me_ref[0]
    seqs = devices * seq_count
    slots = devices * capacity
    items, kinds, _, target = read_ids(ids_ref, devices, seq_count, span, row_counts)
    owner, row = owner_and_row(items, kinds, row_counts)
    fields = jnp.concatenate(
        [
            jnp.where(owner == me, kinds, 4).astype(F32).astype(BF16),
            (row >> 7).astype(F32).astype(BF16),
            (row & 127).astype(F32).astype(BF16),
        ],
        axis=1,
    )
    moves = onehot(target == iota((seqs, seqs), 1))
    moved = dot(moves, fields, TN)
    m_kind = moved[:, :span]
    m_row = moved[:, span : 2 * span] * 128.0 + moved[:, 2 * span : 3 * span]
    hits = jnp.concatenate([onehot(m_kind == float(which)) for which in range(4)], axis=0)
    earlier = onehot(iota((span, span), 0) < iota((span, span), 1))
    ahead = dot(hits, earlier)
    totals = jnp.sum(hits.astype(F32), axis=1, keepdims=True)
    si, sj = iota((seqs, seqs), 0), iota((seqs, seqs), 1)
    sibling = (floor_div(si, seq_count) == floor_div(sj, seq_count)) & (sj < si)
    code = jnp.full((seqs, span), -1.0, F32)
    for which in range(4):
        lo, hi = which * seqs, (which + 1) * seqs
        total = jnp.broadcast_to(totals[lo:hi], (seqs, 128)).astype(BF16)
        shift = dot(onehot(sibling), total)[:, 0:1]
        code = jnp.where(
            m_kind == float(which), ahead[lo:hi] + shift + float(which * capacity), code
        )
    asked = jnp.zeros((seqs, 128), F32)
    lane = iota((seqs, 128), 1)
    for tk in range(4 * capacity):
        value = jnp.sum(jnp.where(code == float(tk), m_row, 0.0), axis=1, keepdims=True)
        asked = jnp.where(lane == tk, value, asked)
    asked_high = jnp.floor(asked * (1.0 / 128.0))
    asked_low = asked - asked_high * 128.0
    spread = onehot(
        floor_div(iota((slots, seqs), 0), capacity) == floor_div(iota((slots, seqs), 1), seq_count)
    )
    full = dot(spread, asked_high.astype(BF16)) * 128.0 + dot(spread, asked_low.astype(BF16))
    place = iota((slots, 128), 0)
    place = place - floor_div(place, capacity) * capacity
    wide = iota((slots, 128), 1)
    columns = jnp.zeros((slots, 128), F32)
    highs, lows = [], []
    for which in range(4):
        index = jnp.sum(
            jnp.where(wide == place + which * capacity, full, 0.0), axis=1, keepdims=True
        )
        high = jnp.floor(index * (1.0 / SPLIT))
        low = index - high * SPLIT
        highs.append(high)
        lows.append(low)
        columns = jnp.where(wide == which, high, columns)
        columns = jnp.where(wide == which + 4, low, columns)
    idxc_ref[...] = columns
    for copy in copies:
        copy.wait()
    low_lane = iota((slots, SPLIT), 1)

    def pick(which):
        return onehot(low_lane == lows[which].astype(jnp.int32))

    narrow = []
    for which in range(2):
        width = widths[which]
        steps = row_counts[which] // SPLIT
        group = 256 // width
        while steps % group:
            group //= 2
        chosen = pick(which)
        block = iota((slots, group * width), 1) >> log2(width)
        total = jnp.zeros((slots, group * width), F32)
        for g in range(steps // group):
            stack = jnp.concatenate(
                [
                    held[which][:, (g * group + b) * SPLIT : (g * group + b + 1) * SPLIT]
                    for b in range(group)
                ],
                axis=0,
            )
            found = dot(chosen, stack, NT)
            total = jnp.where(
                block + g * group == highs[which].astype(jnp.int32), found, total
            )
        folded = total[:, :128]
        for b in range(1, group * width // 128):
            folded = folded + total[:, b * 128 : (b + 1) * 128]
        folded = folded + pltpu.roll(folded, 64, 1)
        narrow.append(folded)
    rows_scr[0] = jnp.where(iota((slots, 128), 1) < widths[0], narrow[0], narrow[1])
    for which in range(2, 4):
        width = widths[which]
        chosen = pick(which)
        total = jnp.zeros((slots, width), F32)
        for step in range(row_counts[which] // SPLIT):
            found = dot(chosen, held[which][step * SPLIT : (step + 1) * SPLIT, :])
            total = jnp.where(highs[which] == float(step), found, total)
        for b in range(width // 128):
            rows_scr[which - 1 + b] = total[:, b * 128 : (b + 1) * 128]

    def pack(device, carry):
        for j in range(4):
            pack_scr[device, j * capacity : (j + 1) * capacity, :] = rows_scr[
                j, pl.ds(device * capacity, capacity), :
            ]
        return carry

    lax.fori_loop(0, devices, pack, 0)
    send_ref[...] = pack_scr[...].astype(BF16)


def layer_kernel(
    devices, seq_count, span, capacity, widths, dp_count, seq_a, seq_b, pieces, *refs
):
    me_ref, got_ref, info_ref, infot_ref, cot_ref = refs[:5]
    refs = refs[5:]
    a_refs, refs = refs[:pieces], refs[pieces:]
    b_refs, refs = refs[:pieces], refs[pieces:]
    out_ref, back_ref = refs[:2]
    pairs, refs = refs[2:6], refs[6:]
    (
        wa, wb, slot_scr, pack_scr, cat_scr, norm_scr, act_scr, slope_scr, attn_scr, tilt_scr,
        att_scr, datt_scr, dproj_scr, gated_scr, og_scr, demb_scr, drow_scr, dact_scr,
        grad_scr, cot_scr, out_scr, back_scr, w_sems, io_sems,
    ) = refs
    dp = me_ref[1]
    width = out_ref.shape[2]
    slots = devices * capacity
    toks = seq_count * span
    rows_each = width // dp_count
    head_dim = width // HEADS
    scale = head_dim**-0.5
    fetches = []
    for refs_in, held, seq in ((b_refs, wb, seq_b), (a_refs, wa, seq_a)):
        index = 0
        for ref in refs_in:
            for k in range(ref.shape[0]):
                start = pl.multiple_of((dp ^ mask_of(index, seq)) * rows_each, rows_each)
                fetches.append(
                    pltpu.make_async_copy(
                        ref.at[k], held.at[pl.ds(start, rows_each), :], w_sems.at[len(fetches)]
                    )
                )
                index += 1
    fetches.append(pltpu.make_async_copy(cot_ref, cot_scr, io_sems.at[0]))
    for copy in fetches:
        copy.start()
    pack_scr[...] = got_ref[...].astype(F32)

    def unpack(device, carry):
        for j in range(4):
            slot_scr[j, pl.ds(device * capacity, capacity), :] = pack_scr[
                device, j * capacity : (j + 1) * capacity, :
            ]
        return carry

    lax.fori_loop(0, devices, unpack, 0)
    arrived = jnp.concatenate([slot_scr[j].astype(BF16) for j in range(4)], axis=1)

    def in_part(j):
        return wa[:, j * width : (j + 1) * width] if j < 3 else wb[:, :width]

    lane = iota((span, width), 1)
    kind_of_lane = jnp.zeros((span, width), jnp.int32)
    edge = 0
    for which in range(3):
        edge += widths[which]
        kind_of_lane = kind_of_lane + jnp.where(lane >= edge, 1, 0)
    blocks = span // 128
    heads = [slice(head * head_dim, (head + 1) * head_dim) for head in range(HEADS)]
    for copy in fetches:
        copy.wait()

    def out_copy(q):
        return pltpu.make_async_copy(out_scr.at[q], out_ref.at[q], io_sems.at[2 + q])

    def sequence(q, carry):
        base = pl.multiple_of(q * span, span)
        rows = pl.ds(base, span)
        slot = infot_ref[rows, 0:1].astype(jnp.int32)
        kind = infot_ref[rows, 1:2].astype(jnp.int32)
        valid = infot_ref[rows, 2:3]
        length = carry_len(q, info_ref, span)
        chosen = onehot(iota((span, slots), 1) == slot)
        cat = jnp.where(kind_of_lane == kind, dot(chosen, arrived), 0.0).astype(BF16)
        cat_scr[rows, :] = cat
        emb = dot(cat, wb[:, 2 * width : 3 * width]).astype(BF16).astype(F32)
        centred = emb - jnp.mean(emb, axis=1, keepdims=True)
        inv = lax.rsqrt(jnp.mean(centred * centred, axis=1, keepdims=True) + 1e-05)
        normed = centred * inv
        norm_scr[rows, :] = normed.astype(BF16)
        for j in (2, 3, 1, 0):
            lean = dot(norm_scr[rows, :], in_part(j)) * 0.5
            twice = jnp.tanh(lean) + 1.0
            part = lean * twice
            act_scr[j] = part.astype(BF16)
            slope_scr[j] = twice + part * (2.0 - twice)
        order = [(rb, head) for rb in range(blocks) for head in range(HEADS)]

        def scores_of(rb, head):
            keys = (rb + 1) * 128
            return dot(
                act_scr[2, rb * 128 : keys, heads[head]], act_scr[3, :keys, heads[head]], NT
            )

        def attend(rb, head):
            keys = (rb + 1) * 128
            here = slice(rb * 128, keys)
            att_scr[here, heads[head]] = dot(
                attn_scr[head, here, :keys], act_scr[1, :keys, heads[head]]
            )

        ahead = [scores_of(*order[0]), scores_of(*order[1])]
        for step, (rb, head) in enumerate(order):
            keys = (rb + 1) * 128
            here = slice(rb * 128, keys)
            if step + 2 < len(order):
                ahead.append(scores_of(*order[step + 2]))
            lean = ahead.pop(0) * (0.5 * scale)
            twice = jnp.tanh(lean) + 1.0
            attn = lean * twice
            key_pos = iota((128, keys), 1)
            keep = (key_pos <= iota((128, keys), 0) + rb * 128) & (key_pos < length)
            attn_scr[head, here, :keys] = jnp.where(keep, attn, 0.0).astype(BF16)
            tilt_scr[head, here, :keys] = jnp.where(
                keep, (twice + attn * (2.0 - twice)) * (0.5 * scale), 0.0
            )
            if step:
                attend(*order[step - 1])
        attend(*order[-1])
        attended = att_scr[...]
        att_c = attended - jnp.mean(attended, axis=1, keepdims=True)
        att_inv = lax.rsqrt(jnp.mean(att_c * att_c, axis=1, keepdims=True) + 1e-05)
        att_n = att_c * att_inv
        gate = act_scr[0].astype(F32)
        gated = (att_n * gate).astype(BF16)
        gated_scr[rows, :] = gated
        out_w = wb[:, width : 2 * width]
        og = jnp.where(valid > 0.5, cot_scr[q].astype(F32), 0.0).astype(BF16)
        og_scr[rows, :] = og
        d_gated = dot(og, out_w, NT).astype(BF16).astype(F32)
        out_scr[q] = (emb + dot(gated, out_w)).astype(BF16)
        out_copy(q).start()
        d_gate = (d_gated * att_n).astype(BF16).astype(F32)
        dproj_scr[rows, :width] = (d_gate * slope_scr[0]).astype(BF16)
        d_n = d_gated * gate
        d_att = att_inv * (
            d_n
            - jnp.mean(d_n, axis=1, keepdims=True)
            - att_n * jnp.mean(d_n * att_n, axis=1, keepdims=True)
        )
        datt_scr[...] = d_att.astype(BF16)
        order = [(rb, head) for rb in reversed(range(blocks)) for head in range(HEADS)]

        def d_attn_of(rb, head):
            keys = (rb + 1) * 128
            return dot(
                datt_scr[rb * 128 : keys, heads[head]], act_scr[1, :keys, heads[head]], NT
            )

        def put(which, rb, head, grad):
            here = slice(rb * 128, (rb + 1) * 128)
            low = which * width + head * head_dim
            dproj_scr[pl.ds(base + rb * 128, 128), low : low + head_dim] = (
                grad.astype(BF16).astype(F32) * slope_scr[which, here, heads[head]]
            ).astype(BF16)

        def settle(rb, head):
            keys = (rb + 1) * 128
            here = slice(rb * 128, keys)
            rest = slice(rb * 128, span)
            cols = heads[head]
            put(2, rb, head, dot(dact_scr[head, here, :keys], act_scr[3, :keys, cols]))
            put(3, rb, head, dot(dact_scr[head, rest, here], act_scr[2, rest, cols], TN))

        ahead = [d_attn_of(*order[0]), d_attn_of(*order[1])]
        for step, (rb, head) in enumerate(order):
            keys = (rb + 1) * 128
            here = slice(rb * 128, keys)
            rest = slice(rb * 128, span)
            if step + 2 < len(order):
                ahead.append(d_attn_of(*order[step + 2]))
            put(1, rb, head, dot(attn_scr[head, rest, here], datt_scr[rest, heads[head]], TN))
            d_attn = ahead.pop(0).astype(BF16).astype(F32)
            dact_scr[head, here, :keys] = (d_attn * tilt_scr[head, here, :keys]).astype(BF16)
            if step:
                settle(*order[step - 1])
        settle(*order[-1])
        d_normed = jnp.zeros((span, width), F32)
        for j in (0, 1, 2, 3):
            d_normed = d_normed + dot(
                dproj_scr[rows, j * width : (j + 1) * width], in_part(j), NT
            )
        d_normed = (d_normed * 0.5).astype(BF16).astype(F32)
        d_emb = inv * (
            d_normed
            - jnp.mean(d_normed, axis=1, keepdims=True)
            - normed * jnp.mean(d_normed * normed, axis=1, keepdims=True)
        )
        d_emb = (d_emb + og.astype(F32)).astype(BF16)
        demb_scr[rows, :] = d_emb
        d_rows = dot(d_emb, wb[:, 2 * width : 3 * width], NT)
        drow_scr[rows, :] = jnp.where(kind_of_lane == kind, d_rows, 0.0).astype(BF16)
        return carry

    lax.fori_loop(0, seq_count, sequence, 0)
    chosen = onehot(iota((slots, toks), 0) == info_ref[0:1, :].astype(jnp.int32))
    outgoing = dot(chosen, drow_scr[...])
    for j in range(4):
        slot_scr[j] = outgoing[:, j * 128 : (j + 1) * 128]

    def pack(device, carry):
        for j in range(4):
            pack_scr[device, j * capacity : (j + 1) * capacity, :] = slot_scr[
                j, pl.ds(device * capacity, capacity), :
            ]
        return carry

    lax.fori_loop(0, devices, pack, 0)
    back_scr[...] = pack_scr[...].astype(BF16)
    back_copy = pltpu.make_async_copy(back_scr, back_ref, io_sems.at[1])
    back_copy.start()
    middle = dp_count // 2

    def emit(block, grad):
        side, place = divmod(block, 3)
        grad_scr[block] = grad.astype(BF16)
        for index in range(dp_count):
            chunk = dp ^ mask_of(index, (seq_a, seq_b)[side])
            rows = pl.ds(pl.multiple_of(chunk * rows_each, rows_each), rows_each)
            pairs[2 * side + index // middle][
                index % middle, :, place * width : (place + 1) * width
            ] = grad_scr[block, rows, :]

    for j in range(4):
        grad = dot(norm_scr[...], dproj_scr[:, j * width : (j + 1) * width], TN)
        emit(j, grad * 0.5)
    emit(4, dot(gated_scr[...], og_scr[...], TN))
    emit(5, dot(cat_scr[...], demb_scr[...], TN))
    for q in range(seq_count):
        out_copy(q).wait()
    back_copy.wait()


def carry_len(q, info_ref, span):
    flags = info_ref[2:3, pl.ds(pl.multiple_of(q * span, 128), span)]
    return jnp.sum(flags, axis=1, keepdims=True).astype(jnp.int32)


def scatter_kernel(devices, capacity, row_counts, widths, *refs):
    got_ref, idxc_ref, idxr_ref = refs[:3]
    outs = refs[3:7]
    held = refs[7:11]
    slot_scr, pack_scr, sems = refs[11:]
    slots = devices * capacity
    pack_scr[...] = got_ref[...].astype(F32)

    def unpack(device, carry):
        for j in range(4):
            slot_scr[j, pl.ds(device * capacity, capacity), :] = pack_scr[
                device, j * capacity : (j + 1) * capacity, :
            ]
        return carry

    lax.fori_loop(0, devices, unpack, 0)
    copies = [pltpu.make_async_copy(held[i], outs[i], sems.at[i]) for i in range(4)]
    first = slot_scr[0]
    rolled = pltpu.roll(first, 64, 1)
    left = iota((slots, 128), 1) < widths[0]
    pairs = [jnp.where(left, first, rolled), jnp.where(left, rolled, first)]
    for which in range(2):
        width = widths[which]
        steps = row_counts[which] // SPLIT
        group = 256 // width
        while steps % group:
            group //= 2
        span = group * width
        high = idxc_ref[:, which : which + 1].astype(jnp.int32)
        low = idxc_ref[:, 4 + which : 5 + which].astype(jnp.int32)
        chosen = onehot(iota((slots, SPLIT), 1) == low)
        wide = jnp.concatenate([pairs[which]] * (span // 128), axis=1)
        block = iota((slots, span), 1) >> log2(width)
        for g in range(steps // group):
            part = jnp.where(block + g * group == high, wide, 0.0).astype(BF16)
            found = dot(part, chosen, TN).astype(BF16)
            for b in range(group):
                at = (g * group + b) * SPLIT
                held[which][:, at : at + SPLIT] = found[b * width : (b + 1) * width, :]
        copies[which].start()
    for which in range(2, 4):
        width = widths[which]
        steps = row_counts[which] // SPLIT
        group = 256 // width
        while steps % group:
            group //= 2
        high = idxc_ref[:, which : which + 1].astype(jnp.int32)
        low = idxr_ref[4 + which : 5 + which, :].astype(jnp.int32)
        chosen = onehot(iota((SPLIT, slots), 0) == low)
        wide = jnp.concatenate(
            [slot_scr[which - 1 + b] for b in range(width // 128)], axis=1
        )
        for g in range(steps // group):
            part = jnp.concatenate(
                [jnp.where(high == g * group + b, wide, 0.0).astype(BF16) for b in range(group)],
                axis=1,
            )
            found = dot(chosen, part).astype(BF16)
            for b in range(group):
                at = (g * group + b) * SPLIT
                held[which][at : at + SPLIT, :] = found[:, b * width : (b + 1) * width]
        copies[which].start()
    for copy in copies:
        copy.wait()


def join_kernel(planes, width, me_ref, *refs):
    parts = refs[:planes]
    proj_ref, in_ref, out_ref, scr = refs[planes:]
    size = parts[0].shape[1]
    for m in range(planes):
        at = pl.multiple_of((me_ref[2] ^ m) * size, 128)
        scr[:, pl.ds(at, size)] = parts[m][...].astype(F32)
    in_ref[...] = scr[:, : 4 * width]
    out_ref[...] = scr[:, 4 * width : 5 * width]
    proj_ref[...] = scr[:, 5 * width :]


def exchange(value, axis, mask):
    count = lax.axis_size(axis)
    return lax.ppermute(value, axis, [(i, i ^ mask) for i in range(count)])


def params(mib):
    return pltpu.CompilerParams(vmem_limit_bytes=mib * 1024 * 1024)


def step(
    item_ids, table_ids, lengths, assignment, table_a, table_b, table_c, table_d,
    proj_weight, in_weight, out_weight, cotangent,
):
    tables = (table_a, table_b, table_c, table_d)
    dp_count = lax.axis_size("dp")
    planes = lax.axis_size("table")
    devices = dp_count * planes
    seq_count, span = item_ids.shape
    toks = seq_count * span
    width = cotangent.shape[2]
    capacity = max(2, toks // (2 * devices))
    slots = devices * capacity
    row_counts = tuple(piece.shape[0] for piece in tables)
    widths = tuple(piece.shape[1] for piece in tables)
    rows_each = width // dp_count
    dp_bits = log2(dp_count)
    dp = lax.axis_index("dp")
    plane = lax.axis_index("table")
    me = jnp.stack([dp * planes + plane, dp, plane]).astype(jnp.int32)
    half = 3 * width
    far = list(range(1, dp_bits))
    seq_a = [0] + far
    seq_b = [0] + far[::-1]
    lanes = span // 128 + 1
    packed = pl.pallas_call(
        functools.partial(key_kernel, devices, row_counts),
        out_shape=jax.ShapeDtypeStruct((devices, seq_count * lanes, 128), jnp.int32),
        in_specs=[SM, SM, VM, VM],
        out_specs=VM,
        compiler_params=params(60),
        name="key",
    )(lengths, assignment, item_ids, table_ids)
    packed, in_weight, out_weight, proj_weight = lax.optimization_barrier(
        (packed, in_weight, out_weight, proj_weight)
    )
    ids = lax.all_to_all(packed, ("dp", "table"), 0, 0, tiled=True)
    own_a = in_weight[:, :half][None]
    own_b = jnp.concatenate([in_weight[:, half:], out_weight, proj_weight], axis=1)[None]

    def gather(held, taken, seq):
        bits = seq[:0:-1]
        for place, bit in enumerate(bits):
            if place:
                taken = exchange(held, "dp", 1 << bit)
            held = jnp.concatenate([held, taken], axis=0)
        return held

    first_a = exchange(own_a, "dp", 1 << seq_a[-1])
    first_b = exchange(own_b, "dp", 1 << seq_b[-1])
    send, idxc = pl.pallas_call(
        functools.partial(
            plan_kernel, devices, seq_count, span, capacity, row_counts, widths
        ),
        out_shape=(
            jax.ShapeDtypeStruct((devices, 4 * capacity, 128), BF16),
            jax.ShapeDtypeStruct((slots, 128), F32),
        ),
        in_specs=[SM, VM] + [HB] * 4,
        out_specs=(VM,) * 2,
        scratch_shapes=[
            pltpu.VMEM((widths[0], row_counts[0]), BF16),
            pltpu.VMEM((widths[1], row_counts[1]), BF16),
            pltpu.VMEM((row_counts[2], widths[2]), BF16),
            pltpu.VMEM((row_counts[3], widths[3]), BF16),
            pltpu.VMEM((4, slots, 128), F32),
            pltpu.VMEM((devices, 4 * capacity, 128), F32),
            pltpu.SemaphoreType.DMA((4,)),
        ],
        compiler_params=params(60),
        name="plan",
    )(me, ids, table_a.T, table_b.T, table_c, table_d)
    send, first_a, first_b = lax.optimization_barrier((send, first_a, first_b))
    near_a = gather(own_a, first_a, seq_a)
    near_b = gather(own_b, first_b, seq_b)
    got = lax.all_to_all(send, ("dp", "table"), 0, 0, tiled=True)
    wa = (near_a, exchange(near_a, "dp", 1 << seq_a[0]))
    wb = (near_b, exchange(near_b, "dp", 1 << seq_b[0]))
    idxr, info, infot = pl.pallas_call(
        functools.partial(own_kernel, devices, seq_count, span, capacity, row_counts),
        out_shape=(
            jax.ShapeDtypeStruct((128, slots), F32),
            jax.ShapeDtypeStruct((8, toks), F32),
            jax.ShapeDtypeStruct((toks, 128), F32),
        ),
        in_specs=[SM, VM, VM],
        out_specs=(VM,) * 3,
        compiler_params=params(16),
        name="own",
    )(me, ids, idxc)
    pieces = len(wa)
    output, back, *pairs = pl.pallas_call(
        functools.partial(
            layer_kernel, devices, seq_count, span, capacity, widths, dp_count, seq_a, seq_b,
            pieces,
        ),
        out_shape=(
            jax.ShapeDtypeStruct((seq_count, span, width), BF16),
            jax.ShapeDtypeStruct((devices, 4 * capacity, 128), BF16),
        )
        + (jax.ShapeDtypeStruct((dp_count // 2, rows_each, half), BF16),) * 4,
        in_specs=[SM] + [VM] * 3 + [HB] * (1 + 2 * pieces),
        out_specs=(HB, HB) + (VM,) * 4,
        scratch_shapes=[
            pltpu.VMEM((width, half), BF16),
            pltpu.VMEM((width, half), BF16),
            pltpu.VMEM((4, slots, 128), F32),
            pltpu.VMEM((devices, 4 * capacity, 128), F32),
            pltpu.VMEM((toks, width), BF16),
            pltpu.VMEM((toks, width), BF16),
            pltpu.VMEM((4, span, width), BF16),
            pltpu.VMEM((4, span, width), F32),
            pltpu.VMEM((HEADS, span, span), BF16),
            pltpu.VMEM((HEADS, span, span), F32),
            pltpu.VMEM((span, width), F32),
            pltpu.VMEM((span, width), BF16),
            pltpu.VMEM((toks, 4 * width), BF16),
            pltpu.VMEM((toks, width), BF16),
            pltpu.VMEM((toks, width), BF16),
            pltpu.VMEM((toks, width), BF16),
            pltpu.VMEM((toks, width), BF16),
            pltpu.VMEM((HEADS, span, span), BF16),
            pltpu.VMEM((6, width, width), BF16),
            pltpu.VMEM((seq_count, span, width), BF16),
            pltpu.VMEM((seq_count, span, width), BF16),
            pltpu.VMEM((devices, 4 * capacity, 128), BF16),
            pltpu.SemaphoreType.DMA((2 * dp_count,)),
            pltpu.SemaphoreType.DMA((2 + seq_count,)),
        ],
        compiler_params=params(48),
        name="layer",
    )(me, got, info, infot, cotangent, *wa, *wb)

    size = 2 * half // planes

    def add(left, right):
        return (left.astype(F32) + right.astype(F32)).astype(BF16)

    returned = lax.all_to_all(back, ("dp", "table"), 0, 0, tiled=True)
    parts = []
    for side, seq in enumerate((seq_a, seq_b)):
        keep, send = pairs[2 * side], pairs[2 * side + 1]
        for place, bit in enumerate(seq):
            taken = exchange(send, "dp", 1 << bit)
            if place < len(seq) - 1:
                mid = keep.shape[0] // 2
                send = add(keep[mid:], taken[mid:])
                keep = add(keep[:mid], taken[:mid])
        for low in range(0, half, size):
            parts.append(add(keep[0, :, low : low + size], taken[0, :, low : low + size]))
    parts = jnp.stack(parts)
    own = [lax.dynamic_index_in_dim(parts, plane ^ m, 0, False) for m in range(planes)]
    total = own[0].astype(F32)
    for m in range(1, planes):
        total = total + exchange(own[m], "table", m).astype(F32)
    summed = total.astype(BF16)
    whole = [summed]
    for m in range(1, planes):
        whole.append(exchange(summed, "table", m))
    grad_proj, grad_in, grad_out = pl.pallas_call(
        functools.partial(join_kernel, planes, width),
        out_shape=(
            jax.ShapeDtypeStruct((rows_each, width), F32),
            jax.ShapeDtypeStruct((rows_each, 4 * width), F32),
            jax.ShapeDtypeStruct((rows_each, width), F32),
        ),
        in_specs=[SM] + [VM] * planes,
        out_specs=(VM,) * 3,
        scratch_shapes=[pltpu.VMEM((rows_each, 2 * half), F32)],
        compiler_params=params(6),
        name="join",
    )(me, *whole)
    g_a, g_b, g_c, g_d = pl.pallas_call(
        functools.partial(scatter_kernel, devices, capacity, row_counts, widths),
        out_shape=(
            jax.ShapeDtypeStruct((widths[0], row_counts[0]), BF16),
            jax.ShapeDtypeStruct((widths[1], row_counts[1]), BF16),
            jax.ShapeDtypeStruct((row_counts[2], widths[2]), BF16),
            jax.ShapeDtypeStruct((row_counts[3], widths[3]), BF16),
        ),
        in_specs=[VM] * 3,
        out_specs=(HB,) * 4,
        scratch_shapes=[
            pltpu.VMEM((widths[0], row_counts[0]), BF16),
            pltpu.VMEM((widths[1], row_counts[1]), BF16),
            pltpu.VMEM((row_counts[2], widths[2]), BF16),
            pltpu.VMEM((row_counts[3], widths[3]), BF16),
            pltpu.VMEM((4, slots, 128), F32),
            pltpu.VMEM((devices, 4 * capacity, 128), F32),
            pltpu.SemaphoreType.DMA((4,)),
        ],
        compiler_params=params(26),
        name="scatter",
    )(returned, idxc, idxr)
    return output, g_a.T, g_b.T, g_c, g_d, grad_proj, grad_in, grad_out


def solution(mesh):
    both = ("dp", "table")
    return jax.shard_map(
        step,
        mesh=mesh,
        in_specs=(
            P(both, None), P(both, None), P(both), P(both),
            P(both, None), P(both, None), P(both, None), P(both, None),
            P("dp", None), P("dp", None), P("dp", None), P(both, None, None),
        ),
        out_specs=(
            P(both, None, None), P(both, None), P(both, None), P(both, None), P(both, None),
            P("dp", None), P("dp", None), P("dp", None),
        ),
        check_vma=False,
    )
```

```python
import functools

import jax
import jax.numpy as jnp
from jax import lax
from jax.experimental import pallas as pl
from jax.experimental.pallas import tpu as pltpu
from jax.sharding import PartitionSpec as P

HEADS = 4
SPLIT = 1024
F32 = jnp.float32
BF16 = jnp.bfloat16
NN = (((1,), (0,)), ((), ()))
NT = (((1,), (1,)), ((), ()))
TN = (((0,), (0,)), ((), ()))
VM = pl.BlockSpec(memory_space=pltpu.VMEM)
SM = pl.BlockSpec(memory_space=pltpu.SMEM)
HB = pl.BlockSpec(memory_space=pl.ANY)


def dot(left, right, dims=NN):
    return lax.dot_general(left, right, dims, preferred_element_type=F32)


def iota(shape, dim):
    return lax.broadcasted_iota(jnp.int32, shape, dim)


def onehot(flags):
    return jnp.where(flags, 1.0, 0.0).astype(BF16)


def floor_div(values, by):
    return jnp.floor((values.astype(F32) + 0.5) * (1.0 / by)).astype(jnp.int32)


def slope_of(twice, part):
    return twice + part * (2.0 - twice)


def log2(value):
    assert value & (value - 1) == 0
    return value.bit_length() - 1


def mask_of(index, seq):
    mask = 0
    for place, bit in enumerate(reversed(seq)):
        if (index >> place) & 1:
            mask |= 1 << bit
    return mask


def owner_and_row(items, kinds, row_counts):
    rows = jnp.zeros_like(items)
    inverse = jnp.zeros(items.shape, F32)
    for which in range(4):
        hit = kinds == which
        rows = jnp.where(hit, row_counts[which], rows)
        inverse = jnp.where(hit, 1.0 / row_counts[which], inverse)
    owner = jnp.floor(items.astype(F32) * inverse).astype(jnp.int32)
    rest = items - owner * rows
    low = rest < 0
    owner = jnp.where(low, owner - 1, owner)
    rest = jnp.where(low, rest + rows, rest)
    high = rest >= rows
    owner = jnp.where(high, owner + 1, owner)
    rest = jnp.where(high, rest - rows, rest)
    return owner, rest


def key_kernel(devices, row_counts, len_ref, to_ref, item_ref, kind_ref, out_ref):
    seq_count, span = item_ref.shape
    keys = item_ref[...]
    kinds = kind_ref[...]
    for which in range(3):
        edge = devices * sum(row_counts[: which + 1])
        keys = jnp.where(kinds == which + 1, item_ref[...] + edge, keys)
    lane = iota((1, 128), 1)
    rows = []
    for q in range(seq_count):
        for c in range(span // 128):
            rows.append(keys[q : q + 1, c * 128 : (c + 1) * 128])
        rows.append(jnp.where(lane == 0, len_ref[q], jnp.where(lane == 1, to_ref[q], 0)))
    block = jnp.concatenate(rows, axis=0)
    out_ref[...] = jnp.broadcast_to(block[None], out_ref.shape)


def read_ids(ids_ref, devices, seq_count, span, row_counts):
    lanes = ids_ref.shape[1] // seq_count
    chunks = span // 128
    keys = jnp.concatenate(
        [
            jnp.concatenate([ids_ref[:, q * lanes + c, :] for c in range(chunks)], axis=1)
            for q in range(seq_count)
        ],
        axis=0,
    )
    tail = jnp.concatenate(
        [ids_ref[:, q * lanes + chunks, :] for q in range(seq_count)], axis=0
    )
    kinds = jnp.zeros_like(keys)
    items = keys
    for which in range(3):
        edge = devices * sum(row_counts[: which + 1])
        kinds = kinds + jnp.where(keys >= edge, 1, 0)
        items = jnp.where(keys >= edge, keys - edge, items)
    lens = tail[:, 0:1]
    target = tail[:, 1:2]
    return items, kinds, lens, target


def own_kernel(devices, seq_count, span, capacity, row_counts, *refs):
    me_ref, ids_ref, idxc_ref, idxr_ref, info_ref, infot_ref = refs
    me = me_ref[0]
    toks = seq_count * span
    idxr_ref[...] = jnp.transpose(idxc_ref[...], (1, 0))
    items, kinds, lens, target = read_ids(ids_ref, devices, seq_count, span, row_counts)
    own_items, own_kinds, own_valid = [], [], []
    for q in range(seq_count):
        hit = target == me * seq_count + q
        own_items.append(jnp.sum(jnp.where(hit, items, 0), axis=0, keepdims=True))
        own_kinds.append(jnp.sum(jnp.where(hit, kinds, 0), axis=0, keepdims=True))
        length = jnp.sum(jnp.where(hit, lens, 0), axis=0, keepdims=True)
        own_valid.append(jnp.where(iota((1, span), 1) < length, 1.0, 0.0))
    e_items = jnp.concatenate(own_items, axis=1)
    e_kinds = jnp.concatenate(own_kinds, axis=1)
    e_valid = jnp.concatenate(own_valid, axis=1)
    e_owner, _ = owner_and_row(e_items, e_kinds, row_counts)
    bucket = e_kinds * devices + e_owner
    member = onehot(iota((4 * devices, toks), 0) == bucket)
    before = onehot(iota((toks, toks), 0) < iota((toks, toks), 1))
    counts = dot(member, before)
    rank = jnp.sum(counts * member.astype(F32), axis=0, keepdims=True)
    slot = e_owner.astype(F32) * capacity + rank
    info = jnp.concatenate([slot, e_kinds.astype(F32), e_valid, jnp.zeros((5, toks), F32)], axis=0)
    info_ref[...] = info
    infot_ref[...] = jnp.transpose(
        jnp.concatenate([info, jnp.zeros((120, toks), F32)], axis=0), (1, 0)
    )


def plan_kernel(devices, seq_count, span, capacity, row_counts, widths, *refs):
    me_ref, ids_ref, refs = refs[0], refs[1], refs[2:]
    table_refs, refs = refs[:4], refs[4:]
    send_ref, idxc_ref = refs[:2]
    held = refs[2:6]
    rows_scr, pack_scr, sems = refs[6:]
    copies = [pltpu.make_async_copy(table_refs[i], held[i], sems.at[i]) for i in range(4)]
    for copy in copies:
        copy.start()
    me = me_ref[0]
    seqs = devices * seq_count
    slots = devices * capacity
    items, kinds, _, target = read_ids(ids_ref, devices, seq_count, span, row_counts)
    owner, row = owner_and_row(items, kinds, row_counts)
    fields = jnp.concatenate(
        [
            jnp.where(owner == me, kinds, 4).astype(F32).astype(BF16),
            (row >> 7).astype(F32).astype(BF16),
            (row & 127).astype(F32).astype(BF16),
        ],
        axis=1,
    )
    moves = onehot(target == iota((seqs, seqs), 1))
    moved = dot(moves, fields, TN)
    m_kind = moved[:, :span]
    m_row = moved[:, span : 2 * span] * 128.0 + moved[:, 2 * span : 3 * span]
    hits = jnp.concatenate([onehot(m_kind == float(which)) for which in range(4)], axis=0)
    earlier = onehot(iota((span, span), 0) < iota((span, span), 1))
    ahead = dot(hits, earlier)
    totals = jnp.sum(hits.astype(F32), axis=1, keepdims=True)
    si, sj = iota((seqs, seqs), 0), iota((seqs, seqs), 1)
    sibling = (floor_div(si, seq_count) == floor_div(sj, seq_count)) & (sj < si)
    code = jnp.full((seqs, span), -1.0, F32)
    for which in range(4):
        lo, hi = which * seqs, (which + 1) * seqs
        total = jnp.broadcast_to(totals[lo:hi], (seqs, 128)).astype(BF16)
        shift = dot(onehot(sibling), total)[:, 0:1]
        code = jnp.where(
            m_kind == float(which), ahead[lo:hi] + shift + float(which * capacity), code
        )
    asked = jnp.zeros((seqs, 128), F32)
    lane = iota((seqs, 128), 1)
    for tk in range(4 * capacity):
        value = jnp.sum(jnp.where(code == float(tk), m_row, 0.0), axis=1, keepdims=True)
        asked = jnp.where(lane == tk, value, asked)
    asked_high = jnp.floor(asked * (1.0 / 128.0))
    asked_low = asked - asked_high * 128.0
    spread = onehot(
        floor_div(iota((slots, seqs), 0), capacity) == floor_div(iota((slots, seqs), 1), seq_count)
    )
    full = dot(spread, asked_high.astype(BF16)) * 128.0 + dot(spread, asked_low.astype(BF16))
    place = iota((slots, 128), 0)
    place = place - floor_div(place, capacity) * capacity
    wide = iota((slots, 128), 1)
    columns = jnp.zeros((slots, 128), F32)
    highs, lows = [], []
    for which in range(4):
        index = jnp.sum(
            jnp.where(wide == place + which * capacity, full, 0.0), axis=1, keepdims=True
        )
        high = jnp.floor(index * (1.0 / SPLIT))
        low = index - high * SPLIT
        highs.append(high)
        lows.append(low)
        columns = jnp.where(wide == which, high, columns)
        columns = jnp.where(wide == which + 4, low, columns)
    idxc_ref[...] = columns
    for copy in copies:
        copy.wait()
    low_lane = iota((slots, SPLIT), 1)

    def pick(which):
        return onehot(low_lane == lows[which].astype(jnp.int32))

    narrow = []
    for which in range(2):
        width = widths[which]
        steps = row_counts[which] // SPLIT
        group = 256 // width
        while steps % group:
            group //= 2
        chosen = pick(which)
        block = iota((slots, group * width), 1) >> log2(width)
        total = jnp.zeros((slots, group * width), F32)
        for g in range(steps // group):
            stack = jnp.concatenate(
                [
                    held[which][:, (g * group + b) * SPLIT : (g * group + b + 1) * SPLIT]
                    for b in range(group)
                ],
                axis=0,
            )
            found = dot(chosen, stack, NT)
            total = jnp.where(
                block + g * group == highs[which].astype(jnp.int32), found, total
            )
        folded = total[:, :128]
        for b in range(1, group * width // 128):
            folded = folded + total[:, b * 128 : (b + 1) * 128]
        folded = folded + pltpu.roll(folded, 64, 1)
        narrow.append(folded)
    rows_scr[0] = jnp.where(iota((slots, 128), 1) < widths[0], narrow[0], narrow[1])
    for which in range(2, 4):
        width = widths[which]
        chosen = pick(which)
        total = jnp.zeros((slots, width), F32)
        for step in range(row_counts[which] // SPLIT):
            found = dot(chosen, held[which][step * SPLIT : (step + 1) * SPLIT, :])
            total = jnp.where(highs[which] == float(step), found, total)
        for b in range(width // 128):
            rows_scr[which - 1 + b] = total[:, b * 128 : (b + 1) * 128]

    def pack(device, carry):
        for j in range(4):
            pack_scr[device, j * capacity : (j + 1) * capacity, :] = rows_scr[
                j, pl.ds(device * capacity, capacity), :
            ]
        return carry

    lax.fori_loop(0, devices, pack, 0)
    send_ref[...] = pack_scr[...].astype(BF16)


def layer_kernel(
    devices, seq_count, span, capacity, widths, dp_count, seq_a, seq_b, pieces, *refs
):
    me_ref, got_ref, info_ref, infot_ref, cot_ref = refs[:5]
    refs = refs[5:]
    a_refs, refs = refs[:pieces], refs[pieces:]
    b_refs, refs = refs[:pieces], refs[pieces:]
    out_ref, back_ref = refs[:2]
    pairs, refs = refs[2:6], refs[6:]
    (
        wa, wb, slot_scr, pack_scr, cat_scr, norm_scr, act_scr, slope_scr, attn_scr, tilt_scr,
        att_scr, datt_scr, dproj_scr, gated_scr, og_scr, demb_scr, drow_scr, dact_scr,
        grad_scr, cot_scr, out_scr, back_scr, keep_scr, w_sems, io_sems,
    ) = refs
    dp = me_ref[1]
    width = out_ref.shape[2]
    slots = devices * capacity
    toks = seq_count * span
    rows_each = width // dp_count
    head_dim = width // HEADS
    scale = head_dim**-0.5
    half_scale = jnp.asarray(0.5 * scale, BF16)
    fetches = []
    for refs_in, held, seq in ((b_refs, wb, seq_b), (a_refs, wa, seq_a)):
        index = 0
        for ref in refs_in:
            for k in range(ref.shape[0]):
                start = pl.multiple_of((dp ^ mask_of(index, seq)) * rows_each, rows_each)
                fetches.append(
                    pltpu.make_async_copy(
                        ref.at[k], held.at[pl.ds(start, rows_each), :], w_sems.at[len(fetches)]
                    )
                )
                index += 1
    fetches.append(pltpu.make_async_copy(cot_ref, cot_scr, io_sems.at[0]))
    for copy in fetches:
        copy.start()
    pack_scr[...] = got_ref[...].astype(F32)

    def unpack(device, carry):
        for j in range(4):
            slot_scr[j, pl.ds(device * capacity, capacity), :] = pack_scr[
                device, j * capacity : (j + 1) * capacity, :
            ]
        return carry

    lax.fori_loop(0, devices, unpack, 0)
    arrived = jnp.concatenate([slot_scr[j].astype(BF16) for j in range(4)], axis=1)

    def in_part(j):
        return wa[:, j * width : (j + 1) * width] if j < 3 else wb[:, :width]

    lane = iota((span, width), 1)
    kind_of_lane = jnp.zeros((span, width), jnp.int32)
    edge = 0
    for which in range(3):
        edge += widths[which]
        kind_of_lane = kind_of_lane + jnp.where(lane >= edge, 1, 0)
    blocks = span // 128
    heads = [slice(head * head_dim, (head + 1) * head_dim) for head in range(HEADS)]
    for copy in fetches:
        copy.wait()

    def out_copy(q):
        return pltpu.make_async_copy(out_scr.at[q], out_ref.at[q], io_sems.at[2 + q])

    def sequence(q, carry):
        base = pl.multiple_of(q * span, span)
        rows = pl.ds(base, span)
        slot = infot_ref[rows, 0:1].astype(jnp.int32)
        kind = infot_ref[rows, 1:2].astype(jnp.int32)
        valid = infot_ref[rows, 2:3]
        inside = info_ref[2:3, pl.ds(base, span)]
        keep_scr[...] = jnp.where(iota((span, span), 1) <= iota((span, span), 0), inside, 0.0)
        chosen = onehot(iota((span, slots), 1) == slot)
        cat = jnp.where(kind_of_lane == kind, dot(chosen, arrived), 0.0).astype(BF16)
        cat_scr[rows, :] = cat
        emb = dot(cat, wb[:, 2 * width : 3 * width]).astype(BF16).astype(F32)
        centred = emb - jnp.mean(emb, axis=1, keepdims=True)
        inv = lax.rsqrt(jnp.mean(centred * centred, axis=1, keepdims=True) + 1e-05)
        normed = centred * inv
        norm_scr[rows, :] = normed.astype(BF16)
        for j in (2, 3, 1, 0):
            lean = dot(norm_scr[rows, :], in_part(j)) * 0.5
            twice = jnp.tanh(lean) + 1.0
            part = (lean * twice).astype(BF16)
            act_scr[j] = part
            slope_scr[j] = slope_of(twice.astype(BF16), part)
        order = [(rb, head) for rb in range(blocks) for head in range(HEADS)]

        def scores_of(rb, head):
            keys = (rb + 1) * 128
            return dot(
                act_scr[2, rb * 128 : keys, heads[head]], act_scr[3, :keys, heads[head]], NT
            )

        def attend(rb, head):
            keys = (rb + 1) * 128
            here = slice(rb * 128, keys)
            att_scr[here, heads[head]] = dot(
                attn_scr[head, here, :keys], act_scr[1, :keys, heads[head]]
            )

        ahead = [scores_of(*order[0]), scores_of(*order[1])]
        for step, (rb, head) in enumerate(order):
            keys = (rb + 1) * 128
            here = slice(rb * 128, keys)
            if step + 2 < len(order):
                ahead.append(scores_of(*order[step + 2]))
            lean = ahead.pop(0) * (0.5 * scale)
            twice = (jnp.tanh(lean) + 1.0) * keep_scr[here, :keys]
            attn = (lean * twice).astype(BF16)
            attn_scr[head, here, :keys] = attn
            tilt_scr[head, here, :keys] = slope_of(twice.astype(BF16), attn) * half_scale
            if step:
                attend(*order[step - 1])
        attend(*order[-1])
        attended = att_scr[...]
        att_c = attended - jnp.mean(attended, axis=1, keepdims=True)
        att_inv = lax.rsqrt(jnp.mean(att_c * att_c, axis=1, keepdims=True) + 1e-05)
        att_n = att_c * att_inv
        gate = act_scr[0].astype(F32)
        gated = (att_n * gate).astype(BF16)
        gated_scr[rows, :] = gated
        out_w = wb[:, width : 2 * width]
        og = jnp.where(valid > 0.5, cot_scr[q].astype(F32), 0.0).astype(BF16)
        og_scr[rows, :] = og
        d_gated = dot(og, out_w, NT).astype(BF16).astype(F32)
        out_scr[q] = (emb + dot(gated, out_w)).astype(BF16)
        out_copy(q).start()
        dproj_scr[rows, :width] = (d_gated * att_n).astype(BF16) * slope_scr[0]
        d_n = d_gated * gate
        d_att = att_inv * (
            d_n
            - jnp.mean(d_n, axis=1, keepdims=True)
            - att_n * jnp.mean(d_n * att_n, axis=1, keepdims=True)
        )
        datt_scr[...] = d_att.astype(BF16)
        order = [(rb, head) for rb in reversed(range(blocks)) for head in range(HEADS)]

        def d_attn_of(rb, head):
            keys = (rb + 1) * 128
            return dot(
                datt_scr[rb * 128 : keys, heads[head]], act_scr[1, :keys, heads[head]], NT
            )

        def put(which, rb, head, grad):
            here = slice(rb * 128, (rb + 1) * 128)
            low = which * width + head * head_dim
            dproj_scr[pl.ds(base + rb * 128, 128), low : low + head_dim] = (
                grad.astype(BF16) * slope_scr[which, here, heads[head]]
            )

        def settle(rb, head):
            keys = (rb + 1) * 128
            here = slice(rb * 128, keys)
            rest = slice(rb * 128, span)
            cols = heads[head]
            put(2, rb, head, dot(dact_scr[head, here, :keys], act_scr[3, :keys, cols]))
            put(3, rb, head, dot(dact_scr[head, rest, here], act_scr[2, rest, cols], TN))

        ahead = [d_attn_of(*order[0]), d_attn_of(*order[1])]
        for step, (rb, head) in enumerate(order):
            keys = (rb + 1) * 128
            here = slice(rb * 128, keys)
            rest = slice(rb * 128, span)
            if step + 2 < len(order):
                ahead.append(d_attn_of(*order[step + 2]))
            put(1, rb, head, dot(attn_scr[head, rest, here], datt_scr[rest, heads[head]], TN))
            dact_scr[head, here, :keys] = (
                ahead.pop(0).astype(BF16) * tilt_scr[head, here, :keys]
            )
            if step:
                settle(*order[step - 1])
        settle(*order[-1])
        d_normed = jnp.zeros((span, width), F32)
        for j in (0, 1, 2, 3):
            d_normed = d_normed + dot(
                dproj_scr[rows, j * width : (j + 1) * width], in_part(j), NT
            )
        d_normed = (d_normed * 0.5).astype(BF16).astype(F32)
        d_emb = inv * (
            d_normed
            - jnp.mean(d_normed, axis=1, keepdims=True)
            - normed * jnp.mean(d_normed * normed, axis=1, keepdims=True)
        )
        d_emb = (d_emb + og.astype(F32)).astype(BF16)
        demb_scr[rows, :] = d_emb
        d_rows = dot(d_emb, wb[:, 2 * width : 3 * width], NT)
        drow_scr[rows, :] = jnp.where(kind_of_lane == kind, d_rows, 0.0).astype(BF16)
        return carry

    lax.fori_loop(0, seq_count, sequence, 0)
    chosen = onehot(iota((slots, toks), 0) == info_ref[0:1, :].astype(jnp.int32))
    outgoing = dot(chosen, drow_scr[...])
    for j in range(4):
        slot_scr[j] = outgoing[:, j * 128 : (j + 1) * 128]

    def pack(device, carry):
        for j in range(4):
            pack_scr[device, j * capacity : (j + 1) * capacity, :] = slot_scr[
                j, pl.ds(device * capacity, capacity), :
            ]
        return carry

    lax.fori_loop(0, devices, pack, 0)
    back_scr[...] = pack_scr[...].astype(BF16)
    back_copy = pltpu.make_async_copy(back_scr, back_ref, io_sems.at[1])
    back_copy.start()
    middle = dp_count // 2

    def emit(block, grad):
        side, place = divmod(block, 3)
        grad_scr[block] = grad.astype(BF16)
        for index in range(dp_count):
            chunk = dp ^ mask_of(index, (seq_a, seq_b)[side])
            rows = pl.ds(pl.multiple_of(chunk * rows_each, rows_each), rows_each)
            pairs[2 * side + index // middle][
                index % middle, :, place * width : (place + 1) * width
            ] = grad_scr[block, rows, :]

    for j in range(4):
        grad = dot(norm_scr[...], dproj_scr[:, j * width : (j + 1) * width], TN)
        emit(j, grad * 0.5)
    emit(4, dot(gated_scr[...], og_scr[...], TN))
    emit(5, dot(cat_scr[...], demb_scr[...], TN))
    for q in range(seq_count):
        out_copy(q).wait()
    back_copy.wait()


def scatter_kernel(devices, capacity, row_counts, widths, *refs):
    got_ref, idxc_ref, idxr_ref = refs[:3]
    outs = refs[3:7]
    held = refs[7:11]
    slot_scr, pack_scr, sems = refs[11:]
    slots = devices * capacity
    pack_scr[...] = got_ref[...].astype(F32)

    def unpack(device, carry):
        for j in range(4):
            slot_scr[j, pl.ds(device * capacity, capacity), :] = pack_scr[
                device, j * capacity : (j + 1) * capacity, :
            ]
        return carry

    lax.fori_loop(0, devices, unpack, 0)
    copies = [pltpu.make_async_copy(held[i], outs[i], sems.at[i]) for i in range(4)]
    first = slot_scr[0]
    rolled = pltpu.roll(first, 64, 1)
    left = iota((slots, 128), 1) < widths[0]
    pairs = [jnp.where(left, first, rolled), jnp.where(left, rolled, first)]
    for which in range(2):
        width = widths[which]
        steps = row_counts[which] // SPLIT
        group = 256 // width
        while steps % group:
            group //= 2
        span = group * width
        high = idxc_ref[:, which : which + 1].astype(jnp.int32)
        low = idxc_ref[:, 4 + which : 5 + which].astype(jnp.int32)
        chosen = onehot(iota((slots, SPLIT), 1) == low)
        wide = jnp.concatenate([pairs[which]] * (span // 128), axis=1)
        block = iota((slots, span), 1) >> log2(width)
        for g in range(steps // group):
            part = jnp.where(block + g * group == high, wide, 0.0).astype(BF16)
            found = dot(part, chosen, TN).astype(BF16)
            for b in range(group):
                at = (g * group + b) * SPLIT
                held[which][:, at : at + SPLIT] = found[b * width : (b + 1) * width, :]
        copies[which].start()
    for which in range(2, 4):
        width = widths[which]
        steps = row_counts[which] // SPLIT
        group = 256 // width
        while steps % group:
            group //= 2
        high = idxc_ref[:, which : which + 1].astype(jnp.int32)
        low = idxr_ref[4 + which : 5 + which, :].astype(jnp.int32)
        chosen = onehot(iota((SPLIT, slots), 0) == low)
        wide = jnp.concatenate(
            [slot_scr[which - 1 + b] for b in range(width // 128)], axis=1
        )
        for g in range(steps // group):
            part = jnp.concatenate(
                [jnp.where(high == g * group + b, wide, 0.0).astype(BF16) for b in range(group)],
                axis=1,
            )
            found = dot(chosen, part).astype(BF16)
            for b in range(group):
                at = (g * group + b) * SPLIT
                held[which][at : at + SPLIT, :] = found[:, b * width : (b + 1) * width]
        copies[which].start()
    for copy in copies:
        copy.wait()


def join_kernel(planes, width, me_ref, *refs):
    parts = refs[:planes]
    proj_ref, in_ref, out_ref, scr = refs[planes:]
    size = parts[0].shape[1]
    for m in range(planes):
        at = pl.multiple_of((me_ref[2] ^ m) * size, 128)
        scr[:, pl.ds(at, size)] = parts[m][...].astype(F32)
    in_ref[...] = scr[:, : 4 * width]
    out_ref[...] = scr[:, 4 * width : 5 * width]
    proj_ref[...] = scr[:, 5 * width :]


def exchange(value, axis, mask):
    count = lax.axis_size(axis)
    return lax.ppermute(value, axis, [(i, i ^ mask) for i in range(count)])


def params(mib):
    return pltpu.CompilerParams(vmem_limit_bytes=mib * 1024 * 1024)


def step(
    item_ids, table_ids, lengths, assignment, table_a, table_b, table_c, table_d,
    proj_weight, in_weight, out_weight, cotangent,
):
    tables = (table_a, table_b, table_c, table_d)
    dp_count = lax.axis_size("dp")
    planes = lax.axis_size("table")
    devices = dp_count * planes
    seq_count, span = item_ids.shape
    toks = seq_count * span
    width = cotangent.shape[2]
    capacity = max(2, toks // (2 * devices))
    slots = devices * capacity
    row_counts = tuple(piece.shape[0] for piece in tables)
    widths = tuple(piece.shape[1] for piece in tables)
    rows_each = width // dp_count
    dp_bits = log2(dp_count)
    dp = lax.axis_index("dp")
    plane = lax.axis_index("table")
    me = jnp.stack([dp * planes + plane, dp, plane]).astype(jnp.int32)
    half = 3 * width
    far = list(range(1, dp_bits))
    seq_a = [0] + far
    seq_b = [0] + far[::-1]
    lanes = span // 128 + 1
    packed = pl.pallas_call(
        functools.partial(key_kernel, devices, row_counts),
        out_shape=jax.ShapeDtypeStruct((devices, seq_count * lanes, 128), jnp.int32),
        in_specs=[SM, SM, VM, VM],
        out_specs=VM,
        compiler_params=params(60),
        name="key",
    )(lengths, assignment, item_ids, table_ids)
    packed, in_weight, out_weight, proj_weight = lax.optimization_barrier(
        (packed, in_weight, out_weight, proj_weight)
    )
    ids = lax.all_to_all(packed, ("dp", "table"), 0, 0, tiled=True)
    own_a = in_weight[:, :half][None]
    own_b = jnp.concatenate([in_weight[:, half:], out_weight, proj_weight], axis=1)[None]

    def gather(held, taken, seq):
        bits = seq[:0:-1]
        for place, bit in enumerate(bits):
            if place:
                taken = exchange(held, "dp", 1 << bit)
            held = jnp.concatenate([held, taken], axis=0)
        return held

    first_a = exchange(own_a, "dp", 1 << seq_a[-1])
    first_b = exchange(own_b, "dp", 1 << seq_b[-1])
    send, idxc = pl.pallas_call(
        functools.partial(
            plan_kernel, devices, seq_count, span, capacity, row_counts, widths
        ),
        out_shape=(
            jax.ShapeDtypeStruct((devices, 4 * capacity, 128), BF16),
            jax.ShapeDtypeStruct((slots, 128), F32),
        ),
        in_specs=[SM, VM] + [HB] * 4,
        out_specs=(VM,) * 2,
        scratch_shapes=[
            pltpu.VMEM((widths[0], row_counts[0]), BF16),
            pltpu.VMEM((widths[1], row_counts[1]), BF16),
            pltpu.VMEM((row_counts[2], widths[2]), BF16),
            pltpu.VMEM((row_counts[3], widths[3]), BF16),
            pltpu.VMEM((4, slots, 128), F32),
            pltpu.VMEM((devices, 4 * capacity, 128), F32),
            pltpu.SemaphoreType.DMA((4,)),
        ],
        compiler_params=params(60),
        name="plan",
    )(me, ids, table_a.T, table_b.T, table_c, table_d)
    send, first_a, first_b = lax.optimization_barrier((send, first_a, first_b))
    near_a = gather(own_a, first_a, seq_a)
    near_b = gather(own_b, first_b, seq_b)
    got = lax.all_to_all(send, ("dp", "table"), 0, 0, tiled=True)
    wa = (near_a, exchange(near_a, "dp", 1 << seq_a[0]))
    wb = (near_b, exchange(near_b, "dp", 1 << seq_b[0]))
    idxr, info, infot = pl.pallas_call(
        functools.partial(own_kernel, devices, seq_count, span, capacity, row_counts),
        out_shape=(
            jax.ShapeDtypeStruct((128, slots), F32),
            jax.ShapeDtypeStruct((8, toks), F32),
            jax.ShapeDtypeStruct((toks, 128), F32),
        ),
        in_specs=[SM, VM, VM],
        out_specs=(VM,) * 3,
        compiler_params=params(16),
        name="own",
    )(me, ids, idxc)
    pieces = len(wa)
    output, back, *pairs = pl.pallas_call(
        functools.partial(
            layer_kernel, devices, seq_count, span, capacity, widths, dp_count, seq_a, seq_b,
            pieces,
        ),
        out_shape=(
            jax.ShapeDtypeStruct((seq_count, span, width), BF16),
            jax.ShapeDtypeStruct((devices, 4 * capacity, 128), BF16),
        )
        + (jax.ShapeDtypeStruct((dp_count // 2, rows_each, half), BF16),) * 4,
        in_specs=[SM] + [VM] * 3 + [HB] * (1 + 2 * pieces),
        out_specs=(HB, HB) + (VM,) * 4,
        scratch_shapes=[
            pltpu.VMEM((width, half), BF16),
            pltpu.VMEM((width, half), BF16),
            pltpu.VMEM((4, slots, 128), F32),
            pltpu.VMEM((devices, 4 * capacity, 128), F32),
            pltpu.VMEM((toks, width), BF16),
            pltpu.VMEM((toks, width), BF16),
            pltpu.VMEM((4, span, width), BF16),
            pltpu.VMEM((4, span, width), BF16),
            pltpu.VMEM((HEADS, span, span), BF16),
            pltpu.VMEM((HEADS, span, span), BF16),
            pltpu.VMEM((span, width), F32),
            pltpu.VMEM((span, width), BF16),
            pltpu.VMEM((toks, 4 * width), BF16),
            pltpu.VMEM((toks, width), BF16),
            pltpu.VMEM((toks, width), BF16),
            pltpu.VMEM((toks, width), BF16),
            pltpu.VMEM((toks, width), BF16),
            pltpu.VMEM((HEADS, span, span), BF16),
            pltpu.VMEM((6, width, width), BF16),
            pltpu.VMEM((seq_count, span, width), BF16),
            pltpu.VMEM((seq_count, span, width), BF16),
            pltpu.VMEM((devices, 4 * capacity, 128), BF16),
            pltpu.VMEM((span, span), F32),
            pltpu.SemaphoreType.DMA((2 * dp_count,)),
            pltpu.SemaphoreType.DMA((2 + seq_count,)),
        ],
        compiler_params=params(48),
        name="layer",
    )(me, got, info, infot, cotangent, *wa, *wb)

    size = 2 * half // planes

    def add(left, right):
        return (left.astype(F32) + right.astype(F32)).astype(BF16)

    returned = lax.all_to_all(back, ("dp", "table"), 0, 0, tiled=True)
    parts = []
    for side, seq in enumerate((seq_a, seq_b)):
        keep, send = pairs[2 * side], pairs[2 * side + 1]
        for place, bit in enumerate(seq):
            taken = exchange(send, "dp", 1 << bit)
            if place < len(seq) - 1:
                mid = keep.shape[0] // 2
                send = add(keep[mid:], taken[mid:])
                keep = add(keep[:mid], taken[:mid])
        for low in range(0, half, size):
            parts.append(add(keep[0, :, low : low + size], taken[0, :, low : low + size]))
    parts = jnp.stack(parts)
    own = [lax.dynamic_index_in_dim(parts, plane ^ m, 0, False) for m in range(planes)]
    total = own[0].astype(F32)
    for m in range(1, planes):
        total = total + exchange(own[m], "table", m).astype(F32)
    summed = total.astype(BF16)
    whole = [summed]
    for m in range(1, planes):
        whole.append(exchange(summed, "table", m))
    grad_proj, grad_in, grad_out = pl.pallas_call(
        functools.partial(join_kernel, planes, width),
        out_shape=(
            jax.ShapeDtypeStruct((rows_each, width), F32),
            jax.ShapeDtypeStruct((rows_each, 4 * width), F32),
            jax.ShapeDtypeStruct((rows_each, width), F32),
        ),
        in_specs=[SM] + [VM] * planes,
        out_specs=(VM,) * 3,
        scratch_shapes=[pltpu.VMEM((rows_each, 2 * half), F32)],
        compiler_params=params(6),
        name="join",
    )(me, *whole)
    g_a, g_b, g_c, g_d = pl.pallas_call(
        functools.partial(scatter_kernel, devices, capacity, row_counts, widths),
        out_shape=(
            jax.ShapeDtypeStruct((widths[0], row_counts[0]), BF16),
            jax.ShapeDtypeStruct((widths[1], row_counts[1]), BF16),
            jax.ShapeDtypeStruct((row_counts[2], widths[2]), BF16),
            jax.ShapeDtypeStruct((row_counts[3], widths[3]), BF16),
        ),
        in_specs=[VM] * 3,
        out_specs=(HB,) * 4,
        scratch_shapes=[
            pltpu.VMEM((widths[0], row_counts[0]), BF16),
            pltpu.VMEM((widths[1], row_counts[1]), BF16),
            pltpu.VMEM((row_counts[2], widths[2]), BF16),
            pltpu.VMEM((row_counts[3], widths[3]), BF16),
            pltpu.VMEM((4, slots, 128), F32),
            pltpu.VMEM((devices, 4 * capacity, 128), F32),
            pltpu.SemaphoreType.DMA((4,)),
        ],
        compiler_params=params(26),
        name="scatter",
    )(returned, idxc, idxr)
    return output, g_a.T, g_b.T, g_c, g_d, grad_proj, grad_in, grad_out


def solution(mesh):
    both = ("dp", "table")
    return jax.shard_map(
        step,
        mesh=mesh,
        in_specs=(
            P(both, None), P(both, None), P(both), P(both),
            P(both, None), P(both, None), P(both, None), P(both, None),
            P("dp", None), P("dp", None), P("dp", None), P(both, None, None),
        ),
        out_specs=(
            P(both, None, None), P(both, None), P(both, None), P(both, None), P(both, None),
            P("dp", None), P("dp", None), P("dp", None),
        ),
        check_vma=False,
    )
```

```python
import functools

import jax
import jax.numpy as jnp
from jax import lax
from jax.experimental import pallas as pl
from jax.experimental.pallas import tpu as pltpu
from jax.sharding import PartitionSpec as P

HEADS = 4
SPLIT = 1024
F32 = jnp.float32
BF16 = jnp.bfloat16
NN = (((1,), (0,)), ((), ()))
NT = (((1,), (1,)), ((), ()))
TN = (((0,), (0,)), ((), ()))
VM = pl.BlockSpec(memory_space=pltpu.VMEM)
SM = pl.BlockSpec(memory_space=pltpu.SMEM)
HB = pl.BlockSpec(memory_space=pl.ANY)


def dot(left, right, dims=NN):
    return lax.dot_general(left, right, dims, preferred_element_type=F32)


def iota(shape, dim):
    return lax.broadcasted_iota(jnp.int32, shape, dim)


def onehot(flags):
    return jnp.where(flags, 1.0, 0.0).astype(BF16)


def floor_div(values, by):
    return jnp.floor((values.astype(F32) + 0.5) * (1.0 / by)).astype(jnp.int32)


def slope_of(twice, part):
    return twice + part * (2.0 - twice)


def log2(value):
    assert value & (value - 1) == 0
    return value.bit_length() - 1


def mask_of(index, seq):
    mask = 0
    for place, bit in enumerate(reversed(seq)):
        if (index >> place) & 1:
            mask |= 1 << bit
    return mask


def owner_and_row(items, kinds, row_counts):
    rows = jnp.zeros_like(items)
    inverse = jnp.zeros(items.shape, F32)
    for which in range(4):
        hit = kinds == which
        rows = jnp.where(hit, row_counts[which], rows)
        inverse = jnp.where(hit, 1.0 / row_counts[which], inverse)
    owner = jnp.floor(items.astype(F32) * inverse).astype(jnp.int32)
    rest = items - owner * rows
    low = rest < 0
    owner = jnp.where(low, owner - 1, owner)
    rest = jnp.where(low, rest + rows, rest)
    high = rest >= rows
    owner = jnp.where(high, owner + 1, owner)
    rest = jnp.where(high, rest - rows, rest)
    return owner, rest


def key_kernel(devices, row_counts, len_ref, to_ref, item_ref, kind_ref, out_ref):
    seq_count, span = item_ref.shape
    keys = item_ref[...]
    kinds = kind_ref[...]
    for which in range(3):
        edge = devices * sum(row_counts[: which + 1])
        keys = jnp.where(kinds == which + 1, item_ref[...] + edge, keys)
    lane = iota((1, 128), 1)
    rows = []
    for q in range(seq_count):
        for c in range(span // 128):
            rows.append(keys[q : q + 1, c * 128 : (c + 1) * 128])
        rows.append(jnp.where(lane == 0, len_ref[q], jnp.where(lane == 1, to_ref[q], 0)))
    block = jnp.concatenate(rows, axis=0)
    out_ref[...] = jnp.broadcast_to(block[None], out_ref.shape)


def read_ids(ids_ref, devices, seq_count, span, row_counts):
    lanes = ids_ref.shape[1] // seq_count
    chunks = span // 128
    keys = jnp.concatenate(
        [
            jnp.concatenate([ids_ref[:, q * lanes + c, :] for c in range(chunks)], axis=1)
            for q in range(seq_count)
        ],
        axis=0,
    )
    tail = jnp.concatenate(
        [ids_ref[:, q * lanes + chunks, :] for q in range(seq_count)], axis=0
    )
    kinds = jnp.zeros_like(keys)
    items = keys
    for which in range(3):
        edge = devices * sum(row_counts[: which + 1])
        kinds = kinds + jnp.where(keys >= edge, 1, 0)
        items = jnp.where(keys >= edge, keys - edge, items)
    lens = tail[:, 0:1]
    target = tail[:, 1:2]
    return items, kinds, lens, target


def own_kernel(devices, seq_count, span, capacity, row_counts, *refs):
    me_ref, ids_ref, idxc_ref, idxr_ref, info_ref, infot_ref = refs
    me = me_ref[0]
    toks = seq_count * span
    idxr_ref[...] = jnp.transpose(idxc_ref[...], (1, 0))
    items, kinds, lens, target = read_ids(ids_ref, devices, seq_count, span, row_counts)
    own_items, own_kinds, own_valid = [], [], []
    for q in range(seq_count):
        hit = target == me * seq_count + q
        own_items.append(jnp.sum(jnp.where(hit, items, 0), axis=0, keepdims=True))
        own_kinds.append(jnp.sum(jnp.where(hit, kinds, 0), axis=0, keepdims=True))
        length = jnp.sum(jnp.where(hit, lens, 0), axis=0, keepdims=True)
        own_valid.append(jnp.where(iota((1, span), 1) < length, 1.0, 0.0))
    e_items = jnp.concatenate(own_items, axis=1)
    e_kinds = jnp.concatenate(own_kinds, axis=1)
    e_valid = jnp.concatenate(own_valid, axis=1)
    e_owner, _ = owner_and_row(e_items, e_kinds, row_counts)
    bucket = e_kinds * devices + e_owner
    member = onehot(iota((4 * devices, toks), 0) == bucket)
    before = onehot(iota((toks, toks), 0) < iota((toks, toks), 1))
    counts = dot(member, before)
    rank = jnp.sum(counts * member.astype(F32), axis=0, keepdims=True)
    slot = e_owner.astype(F32) * capacity + rank
    info = jnp.concatenate([slot, e_kinds.astype(F32), e_valid, jnp.zeros((5, toks), F32)], axis=0)
    info_ref[...] = info
    infot_ref[...] = jnp.transpose(
        jnp.concatenate([info, jnp.zeros((120, toks), F32)], axis=0), (1, 0)
    )


def plan_kernel(devices, seq_count, span, capacity, row_counts, widths, *refs):
    me_ref, ids_ref, refs = refs[0], refs[1], refs[2:]
    table_refs, refs = refs[:4], refs[4:]
    send_ref, idxc_ref = refs[:2]
    held = refs[2:6]
    rows_scr, pack_scr, ids_scr, sems = refs[6:]
    ids_copy = pltpu.make_async_copy(ids_ref, ids_scr, sems.at[4])
    ids_copy.start()
    copies = [pltpu.make_async_copy(table_refs[i], held[i], sems.at[i]) for i in range(4)]
    for copy in copies:
        copy.start()
    me = me_ref[0]
    seqs = devices * seq_count
    slots = devices * capacity
    ids_copy.wait()
    items, kinds, _, target = read_ids(ids_scr, devices, seq_count, span, row_counts)
    owner, row = owner_and_row(items, kinds, row_counts)
    fields = jnp.concatenate(
        [
            jnp.where(owner == me, kinds, 4).astype(F32).astype(BF16),
            (row >> 7).astype(F32).astype(BF16),
            (row & 127).astype(F32).astype(BF16),
        ],
        axis=1,
    )
    moves = onehot(target == iota((seqs, seqs), 1))
    moved = dot(moves, fields, TN)
    m_kind = moved[:, :span]
    m_row = moved[:, span : 2 * span] * 128.0 + moved[:, 2 * span : 3 * span]
    hits = jnp.concatenate([onehot(m_kind == float(which)) for which in range(4)], axis=0)
    earlier = onehot(iota((span, span), 0) < iota((span, span), 1))
    ahead = dot(hits, earlier)
    totals = jnp.sum(hits.astype(F32), axis=1, keepdims=True)
    si, sj = iota((seqs, seqs), 0), iota((seqs, seqs), 1)
    sibling = (floor_div(si, seq_count) == floor_div(sj, seq_count)) & (sj < si)
    code = jnp.full((seqs, span), -1.0, F32)
    for which in range(4):
        lo, hi = which * seqs, (which + 1) * seqs
        total = jnp.broadcast_to(totals[lo:hi], (seqs, 128)).astype(BF16)
        shift = dot(onehot(sibling), total)[:, 0:1]
        code = jnp.where(
            m_kind == float(which), ahead[lo:hi] + shift + float(which * capacity), code
        )
    asked = jnp.zeros((seqs, 128), F32)
    lane = iota((seqs, 128), 1)
    for tk in range(4 * capacity):
        value = jnp.sum(jnp.where(code == float(tk), m_row, 0.0), axis=1, keepdims=True)
        asked = jnp.where(lane == tk, value, asked)
    asked_high = jnp.floor(asked * (1.0 / 128.0))
    asked_low = asked - asked_high * 128.0
    spread = onehot(
        floor_div(iota((slots, seqs), 0), capacity) == floor_div(iota((slots, seqs), 1), seq_count)
    )
    full = dot(spread, asked_high.astype(BF16)) * 128.0 + dot(spread, asked_low.astype(BF16))
    place = iota((slots, 128), 0)
    place = place - floor_div(place, capacity) * capacity
    wide = iota((slots, 128), 1)
    columns = jnp.zeros((slots, 128), F32)
    highs, lows = [], []
    for which in range(4):
        index = jnp.sum(
            jnp.where(wide == place + which * capacity, full, 0.0), axis=1, keepdims=True
        )
        high = jnp.floor(index * (1.0 / SPLIT))
        low = index - high * SPLIT
        highs.append(high)
        lows.append(low)
        columns = jnp.where(wide == which, high, columns)
        columns = jnp.where(wide == which + 4, low, columns)
    idxc_ref[...] = columns
    for copy in copies:
        copy.wait()
    low_lane = iota((slots, SPLIT), 1)

    def pick(which):
        return onehot(low_lane == lows[which].astype(jnp.int32))

    narrow = []
    for which in range(2):
        width = widths[which]
        steps = row_counts[which] // SPLIT
        group = 256 // width
        while steps % group:
            group //= 2
        chosen = pick(which)
        block = iota((slots, group * width), 1) >> log2(width)
        total = jnp.zeros((slots, group * width), F32)
        for g in range(steps // group):
            stack = jnp.concatenate(
                [
                    held[which][:, (g * group + b) * SPLIT : (g * group + b + 1) * SPLIT]
                    for b in range(group)
                ],
                axis=0,
            )
            found = dot(chosen, stack, NT)
            total = jnp.where(
                block + g * group == highs[which].astype(jnp.int32), found, total
            )
        folded = total[:, :128]
        for b in range(1, group * width // 128):
            folded = folded + total[:, b * 128 : (b + 1) * 128]
        folded = folded + pltpu.roll(folded, 64, 1)
        narrow.append(folded)
    rows_scr[0, :slots] = jnp.where(iota((slots, 128), 1) < widths[0], narrow[0], narrow[1])
    for which in range(2, 4):
        width = widths[which]
        chosen = pick(which)
        total = jnp.zeros((slots, width), F32)
        for step in range(row_counts[which] // SPLIT):
            found = dot(chosen, held[which][step * SPLIT : (step + 1) * SPLIT, :])
            total = jnp.where(highs[which] == float(step), found, total)
        for b in range(width // 128):
            rows_scr[which - 1 + b, :slots] = total[:, b * 128 : (b + 1) * 128]

    def pack(device, carry):
        for j in range(4):
            pack_scr[device, j * capacity : (j + 1) * capacity, :] = rows_scr[
                j, pl.ds(device * capacity, capacity), :
            ]
        return carry

    lax.fori_loop(0, devices, pack, 0)
    send_ref[...] = pack_scr[:devices].astype(BF16)


def layer_kernel(
    devices, seq_count, span, capacity, widths, dp_count, seq_a, seq_b, pieces, *refs
):
    me_ref, got_ref, info_ref, infot_ref, cot_ref = refs[:5]
    refs = refs[5:]
    a_refs, refs = refs[:pieces], refs[pieces:]
    b_refs, refs = refs[:pieces], refs[pieces:]
    out_ref, back_ref = refs[:2]
    pairs, refs = refs[2:6], refs[6:]
    (
        wa, wb, slot_scr, pack_scr, cat_scr, norm_scr, act_scr, slope_scr, attn_scr, tilt_scr,
        att_scr, datt_scr, dproj_scr, gated_scr, og_scr, demb_scr, drow_scr, dact_scr,
        grad_scr, cot_scr, out_scr, back_scr, keep_scr, w_sems, io_sems,
    ) = refs
    dp = me_ref[1]
    width = out_ref.shape[2]
    slots = devices * capacity
    toks = seq_count * span
    rows_each = width // dp_count
    head_dim = width // HEADS
    scale = head_dim**-0.5
    half_scale = jnp.asarray(0.5 * scale, BF16)
    fetches = []
    for refs_in, held, seq in ((b_refs, wb, seq_b), (a_refs, wa, seq_a)):
        index = 0
        for ref in refs_in:
            for k in range(ref.shape[0]):
                start = pl.multiple_of((dp ^ mask_of(index, seq)) * rows_each, rows_each)
                fetches.append(
                    pltpu.make_async_copy(
                        ref.at[k], held.at[pl.ds(start, rows_each), :], w_sems.at[len(fetches)]
                    )
                )
                index += 1
    fetches.append(pltpu.make_async_copy(cot_ref, cot_scr, io_sems.at[0]))
    for copy in fetches:
        copy.start()
    pack_scr[:devices] = got_ref[...].astype(F32)

    def unpack(device, carry):
        for j in range(4):
            slot_scr[j, pl.ds(device * capacity, capacity), :] = pack_scr[
                device, j * capacity : (j + 1) * capacity, :
            ]
        return carry

    lax.fori_loop(0, devices, unpack, 0)
    arrived = jnp.concatenate([slot_scr[j, :slots].astype(BF16) for j in range(4)], axis=1)

    def in_part(j):
        return wa[:, j * width : (j + 1) * width] if j < 3 else wb[:, :width]

    lane = iota((span, width), 1)
    kind_of_lane = jnp.zeros((span, width), jnp.int32)
    edge = 0
    for which in range(3):
        edge += widths[which]
        kind_of_lane = kind_of_lane + jnp.where(lane >= edge, 1, 0)
    blocks = span // 128
    heads = [slice(head * head_dim, (head + 1) * head_dim) for head in range(HEADS)]
    for copy in fetches:
        copy.wait()

    def out_copy(q):
        return pltpu.make_async_copy(out_scr.at[q], out_ref.at[q], io_sems.at[2 + q])

    def sequence(q, carry):
        base = pl.multiple_of(q * span, span)
        rows = pl.ds(base, span)
        slot = infot_ref[rows, 0:1].astype(jnp.int32)
        kind = infot_ref[rows, 1:2].astype(jnp.int32)
        valid = infot_ref[rows, 2:3]
        inside = info_ref[2:3, pl.ds(base, span)]
        keep_scr[...] = jnp.where(iota((span, span), 1) <= iota((span, span), 0), inside, 0.0)
        chosen = onehot(iota((span, slots), 1) == slot)
        cat = jnp.where(kind_of_lane == kind, dot(chosen, arrived), 0.0).astype(BF16)
        cat_scr[rows, :] = cat
        emb = dot(cat, wb[:, 2 * width : 3 * width]).astype(BF16).astype(F32)
        centred = emb - jnp.mean(emb, axis=1, keepdims=True)
        inv = lax.rsqrt(jnp.mean(centred * centred, axis=1, keepdims=True) + 1e-05)
        normed = centred * inv
        norm_scr[rows, :] = normed.astype(BF16)
        for j in (2, 3, 1, 0):
            lean = dot(norm_scr[rows, :], in_part(j)) * 0.5
            twice = jnp.tanh(lean) + 1.0
            part = (lean * twice).astype(BF16)
            act_scr[j] = part
            slope_scr[j] = slope_of(twice.astype(BF16), part)
        order = [(rb, head) for rb in range(blocks) for head in range(HEADS)]

        def scores_of(rb, head):
            keys = (rb + 1) * 128
            return dot(
                act_scr[2, rb * 128 : keys, heads[head]], act_scr[3, :keys, heads[head]], NT
            )

        def attend(rb, head):
            keys = (rb + 1) * 128
            here = slice(rb * 128, keys)
            att_scr[here, heads[head]] = dot(
                attn_scr[head, here, :keys], act_scr[1, :keys, heads[head]]
            )

        ahead = [scores_of(*order[0]), scores_of(*order[1])]
        for step, (rb, head) in enumerate(order):
            keys = (rb + 1) * 128
            here = slice(rb * 128, keys)
            if step + 2 < len(order):
                ahead.append(scores_of(*order[step + 2]))
            lean = ahead.pop(0) * (0.5 * scale)
            twice = (jnp.tanh(lean) + 1.0) * keep_scr[here, :keys]
            attn = (lean * twice).astype(BF16)
            attn_scr[head, here, :keys] = attn
            tilt_scr[head, here, :keys] = slope_of(twice.astype(BF16), attn) * half_scale
            if step:
                attend(*order[step - 1])
        attend(*order[-1])
        attended = att_scr[...]
        att_c = attended - jnp.mean(attended, axis=1, keepdims=True)
        att_inv = lax.rsqrt(jnp.mean(att_c * att_c, axis=1, keepdims=True) + 1e-05)
        att_n = att_c * att_inv
        gate = act_scr[0].astype(F32)
        gated = (att_n * gate).astype(BF16)
        gated_scr[rows, :] = gated
        out_w = wb[:, width : 2 * width]
        og = jnp.where(valid > 0.5, cot_scr[q].astype(F32), 0.0).astype(BF16)
        og_scr[rows, :] = og
        d_gated = dot(og, out_w, NT).astype(BF16).astype(F32)
        out_scr[q] = (emb + dot(gated, out_w)).astype(BF16)
        out_copy(q).start()
        dproj_scr[rows, :width] = (d_gated * att_n).astype(BF16) * slope_scr[0]
        d_n = d_gated * gate
        d_att = att_inv * (
            d_n
            - jnp.mean(d_n, axis=1, keepdims=True)
            - att_n * jnp.mean(d_n * att_n, axis=1, keepdims=True)
        )
        datt_scr[...] = d_att.astype(BF16)
        order = [(rb, head) for rb in reversed(range(blocks)) for head in range(HEADS)]

        def d_attn_of(rb, head):
            keys = (rb + 1) * 128
            return dot(
                datt_scr[rb * 128 : keys, heads[head]], act_scr[1, :keys, heads[head]], NT
            )

        def put(which, rb, head, grad):
            here = slice(rb * 128, (rb + 1) * 128)
            low = which * width + head * head_dim
            dproj_scr[pl.ds(base + rb * 128, 128), low : low + head_dim] = (
                grad.astype(BF16) * slope_scr[which, here, heads[head]]
            )

        def settle(rb, head):
            keys = (rb + 1) * 128
            here = slice(rb * 128, keys)
            rest = slice(rb * 128, span)
            cols = heads[head]
            put(2, rb, head, dot(dact_scr[head, here, :keys], act_scr[3, :keys, cols]))
            put(3, rb, head, dot(dact_scr[head, rest, here], act_scr[2, rest, cols], TN))

        ahead = [d_attn_of(*order[0]), d_attn_of(*order[1])]
        for step, (rb, head) in enumerate(order):
            keys = (rb + 1) * 128
            here = slice(rb * 128, keys)
            rest = slice(rb * 128, span)
            if step + 2 < len(order):
                ahead.append(d_attn_of(*order[step + 2]))
            put(1, rb, head, dot(attn_scr[head, rest, here], datt_scr[rest, heads[head]], TN))
            dact_scr[head, here, :keys] = (
                ahead.pop(0).astype(BF16) * tilt_scr[head, here, :keys]
            )
            if step:
                settle(*order[step - 1])
        settle(*order[-1])
        d_normed = jnp.zeros((span, width), F32)
        for j in (0, 1, 2, 3):
            d_normed = d_normed + dot(
                dproj_scr[rows, j * width : (j + 1) * width], in_part(j), NT
            )
        d_normed = (d_normed * 0.5).astype(BF16).astype(F32)
        d_emb = inv * (
            d_normed
            - jnp.mean(d_normed, axis=1, keepdims=True)
            - normed * jnp.mean(d_normed * normed, axis=1, keepdims=True)
        )
        d_emb = (d_emb + og.astype(F32)).astype(BF16)
        demb_scr[rows, :] = d_emb
        d_rows = dot(d_emb, wb[:, 2 * width : 3 * width], NT)
        drow_scr[rows, :] = jnp.where(kind_of_lane == kind, d_rows, 0.0).astype(BF16)
        return carry

    lax.fori_loop(0, seq_count, sequence, 0)
    chosen = onehot(iota((slots, toks), 0) == info_ref[0:1, :].astype(jnp.int32))
    outgoing = dot(chosen, drow_scr[...])
    for j in range(4):
        slot_scr[j, :slots] = outgoing[:, j * 128 : (j + 1) * 128]

    def pack(device, carry):
        for j in range(4):
            pack_scr[device, j * capacity : (j + 1) * capacity, :] = slot_scr[
                j, pl.ds(device * capacity, capacity), :
            ]
        return carry

    lax.fori_loop(0, devices, pack, 0)
    back_scr[...] = pack_scr[:devices].astype(BF16)
    back_copy = pltpu.make_async_copy(back_scr, back_ref, io_sems.at[1])
    back_copy.start()
    middle = dp_count // 2

    def emit(block, grad):
        side, place = divmod(block, 3)
        grad_scr[block] = grad.astype(BF16)
        for index in range(dp_count):
            chunk = dp ^ mask_of(index, (seq_a, seq_b)[side])
            rows = pl.ds(pl.multiple_of(chunk * rows_each, rows_each), rows_each)
            pairs[2 * side + index // middle][
                index % middle, :, place * width : (place + 1) * width
            ] = grad_scr[block, rows, :]

    for j in range(4):
        grad = dot(norm_scr[...], dproj_scr[:, j * width : (j + 1) * width], TN)
        emit(j, grad * 0.5)
    emit(4, dot(gated_scr[...], og_scr[...], TN))
    emit(5, dot(cat_scr[...], demb_scr[...], TN))
    for q in range(seq_count):
        out_copy(q).wait()
    back_copy.wait()


def scatter_kernel(devices, capacity, row_counts, widths, *refs):
    got_ref, idxc_ref, idxr_ref = refs[:3]
    outs = refs[3:7]
    held = refs[7:11]
    slot_scr, pack_scr, sems = refs[11:]
    slots = devices * capacity
    pack_scr[:devices] = got_ref[...].astype(F32)

    def unpack(device, carry):
        for j in range(4):
            slot_scr[j, pl.ds(device * capacity, capacity), :] = pack_scr[
                device, j * capacity : (j + 1) * capacity, :
            ]
        return carry

    lax.fori_loop(0, devices, unpack, 0)
    copies = [pltpu.make_async_copy(held[i], outs[i], sems.at[i]) for i in range(4)]
    first = slot_scr[0, :slots]
    rolled = pltpu.roll(first, 64, 1)
    left = iota((slots, 128), 1) < widths[0]
    pairs = [jnp.where(left, first, rolled), jnp.where(left, rolled, first)]
    for which in range(2):
        width = widths[which]
        steps = row_counts[which] // SPLIT
        group = 256 // width
        while steps % group:
            group //= 2
        span = group * width
        high = idxc_ref[:, which : which + 1].astype(jnp.int32)
        low = idxc_ref[:, 4 + which : 5 + which].astype(jnp.int32)
        chosen = onehot(iota((slots, SPLIT), 1) == low)
        wide = jnp.concatenate([pairs[which]] * (span // 128), axis=1)
        block = iota((slots, span), 1) >> log2(width)
        for g in range(steps // group):
            part = jnp.where(block + g * group == high, wide, 0.0).astype(BF16)
            found = dot(part, chosen, TN).astype(BF16)
            for b in range(group):
                at = (g * group + b) * SPLIT
                held[which][:, at : at + SPLIT] = found[b * width : (b + 1) * width, :]
        copies[which].start()
    for which in range(2, 4):
        width = widths[which]
        steps = row_counts[which] // SPLIT
        group = 256 // width
        while steps % group:
            group //= 2
        high = idxc_ref[:, which : which + 1].astype(jnp.int32)
        low = idxr_ref[4 + which : 5 + which, :].astype(jnp.int32)
        chosen = onehot(iota((SPLIT, slots), 0) == low)
        wide = jnp.concatenate(
            [slot_scr[which - 1 + b, :slots] for b in range(width // 128)], axis=1
        )
        for g in range(steps // group):
            part = jnp.concatenate(
                [jnp.where(high == g * group + b, wide, 0.0).astype(BF16) for b in range(group)],
                axis=1,
            )
            found = dot(chosen, part).astype(BF16)
            for b in range(group):
                at = (g * group + b) * SPLIT
                held[which][at : at + SPLIT, :] = found[:, b * width : (b + 1) * width]
        copies[which].start()
    for copy in copies:
        copy.wait()


def join_kernel(planes, width, me_ref, *refs):
    parts = refs[:planes]
    proj_ref, in_ref, out_ref, scr = refs[planes:]
    size = parts[0].shape[1]
    for m in range(planes):
        at = pl.multiple_of((me_ref[2] ^ m) * size, 128)
        scr[:, pl.ds(at, size)] = parts[m][...].astype(F32)
    in_ref[...] = scr[:, : 4 * width]
    out_ref[...] = scr[:, 4 * width : 5 * width]
    proj_ref[...] = scr[:, 5 * width :]


def exchange(value, axis, mask):
    count = lax.axis_size(axis)
    return lax.ppermute(value, axis, [(i, i ^ mask) for i in range(count)])


def params(mib):
    return pltpu.CompilerParams(vmem_limit_bytes=mib * 1024 * 1024)


def step(
    item_ids, table_ids, lengths, assignment, table_a, table_b, table_c, table_d,
    proj_weight, in_weight, out_weight, cotangent,
):
    tables = (table_a, table_b, table_c, table_d)
    dp_count = lax.axis_size("dp")
    planes = lax.axis_size("table")
    devices = dp_count * planes
    seq_count, span = item_ids.shape
    toks = seq_count * span
    width = cotangent.shape[2]
    capacity = max(2, toks // (2 * devices))
    slots = devices * capacity
    row_counts = tuple(piece.shape[0] for piece in tables)
    widths = tuple(piece.shape[1] for piece in tables)
    rows_each = width // dp_count
    dp_bits = log2(dp_count)
    dp = lax.axis_index("dp")
    plane = lax.axis_index("table")
    me = jnp.stack([dp * planes + plane, dp, plane]).astype(jnp.int32)
    half = 3 * width
    far = list(range(1, dp_bits))
    seq_a = [0] + far
    seq_b = [0] + far[::-1]
    lanes = span // 128 + 1
    packed = pl.pallas_call(
        functools.partial(key_kernel, devices, row_counts),
        out_shape=jax.ShapeDtypeStruct((devices, seq_count * lanes, 128), jnp.int32),
        in_specs=[SM, SM, VM, VM],
        out_specs=VM,
        compiler_params=params(60),
        name="key",
    )(lengths, assignment, item_ids, table_ids)
    packed, in_weight, out_weight, proj_weight = lax.optimization_barrier(
        (packed, in_weight, out_weight, proj_weight)
    )
    ids = lax.all_to_all(packed, ("dp", "table"), 0, 0, tiled=True)
    own_a = in_weight[:, :half][None]
    own_b = jnp.concatenate([in_weight[:, half:], out_weight, proj_weight], axis=1)[None]

    def gather(held, taken, seq):
        bits = seq[:0:-1]
        for place, bit in enumerate(bits):
            if place:
                taken = exchange(held, "dp", 1 << bit)
            held = jnp.concatenate([held, taken], axis=0)
        return held

    first_a = exchange(own_a, "dp", 1 << seq_a[-1])
    first_b = exchange(own_b, "dp", 1 << seq_b[-1])
    send, idxc = pl.pallas_call(
        functools.partial(
            plan_kernel, devices, seq_count, span, capacity, row_counts, widths
        ),
        out_shape=(
            jax.ShapeDtypeStruct((devices, 4 * capacity, 128), BF16),
            jax.ShapeDtypeStruct((slots, 128), F32),
        ),
        in_specs=[SM, HB] + [HB] * 4,
        out_specs=(VM,) * 2,
        scratch_shapes=[
            pltpu.VMEM((widths[0], row_counts[0]), BF16),
            pltpu.VMEM((widths[1], row_counts[1]), BF16),
            pltpu.VMEM((row_counts[2], widths[2]), BF16),
            pltpu.VMEM((row_counts[3], widths[3]), BF16),
            pltpu.VMEM((4, slots + 8, 128), F32),
            pltpu.VMEM((devices + 1, 4 * capacity, 128), F32),
            pltpu.VMEM((devices, seq_count * lanes, 128), jnp.int32),
            pltpu.SemaphoreType.DMA((5,)),
        ],
        compiler_params=params(60),
        name="plan",
    )(me, ids, table_a.T, table_b.T, table_c, table_d)
    send, first_a, first_b = lax.optimization_barrier((send, first_a, first_b))
    near_a = gather(own_a, first_a, seq_a)
    near_b = gather(own_b, first_b, seq_b)
    got = lax.all_to_all(send, ("dp", "table"), 0, 0, tiled=True)
    wa = (near_a, exchange(near_a, "dp", 1 << seq_a[0]))
    wb = (near_b, exchange(near_b, "dp", 1 << seq_b[0]))
    idxr, info, infot = pl.pallas_call(
        functools.partial(own_kernel, devices, seq_count, span, capacity, row_counts),
        out_shape=(
            jax.ShapeDtypeStruct((128, slots), F32),
            jax.ShapeDtypeStruct((8, toks), F32),
            jax.ShapeDtypeStruct((toks, 128), F32),
        ),
        in_specs=[SM, VM, VM],
        out_specs=(VM,) * 3,
        compiler_params=params(16),
        name="own",
    )(me, ids, idxc)
    pieces = len(wa)
    output, back, *pairs = pl.pallas_call(
        functools.partial(
            layer_kernel, devices, seq_count, span, capacity, widths, dp_count, seq_a, seq_b,
            pieces,
        ),
        out_shape=(
            jax.ShapeDtypeStruct((seq_count, span, width), BF16),
            jax.ShapeDtypeStruct((devices, 4 * capacity, 128), BF16),
        )
        + (jax.ShapeDtypeStruct((dp_count // 2, rows_each, half), BF16),) * 4,
        in_specs=[SM] + [VM] * 3 + [HB] * (1 + 2 * pieces),
        out_specs=(HB, HB) + (VM,) * 4,
        scratch_shapes=[
            pltpu.VMEM((width, half), BF16),
            pltpu.VMEM((width, half), BF16),
            pltpu.VMEM((4, slots + 8, 128), F32),
            pltpu.VMEM((devices + 1, 4 * capacity, 128), F32),
            pltpu.VMEM((toks, width), BF16),
            pltpu.VMEM((toks, width), BF16),
            pltpu.VMEM((4, span, width), BF16),
            pltpu.VMEM((4, span, width), BF16),
            pltpu.VMEM((HEADS, span, span), BF16),
            pltpu.VMEM((HEADS, span, span), BF16),
            pltpu.VMEM((span, width), F32),
            pltpu.VMEM((span, width), BF16),
            pltpu.VMEM((toks, 4 * width), BF16),
            pltpu.VMEM((toks, width), BF16),
            pltpu.VMEM((toks, width), BF16),
            pltpu.VMEM((toks, width), BF16),
            pltpu.VMEM((toks, width), BF16),
            pltpu.VMEM((HEADS, span, span), BF16),
            pltpu.VMEM((6, width, width), BF16),
            pltpu.VMEM((seq_count, span, width), BF16),
            pltpu.VMEM((seq_count, span, width), BF16),
            pltpu.VMEM((devices, 4 * capacity, 128), BF16),
            pltpu.VMEM((span, span), F32),
            pltpu.SemaphoreType.DMA((2 * dp_count,)),
            pltpu.SemaphoreType.DMA((2 + seq_count,)),
        ],
        compiler_params=params(50),
        name="layer",
    )(me, got, info, infot, cotangent, *wa, *wb)

    size = 2 * half // planes

    def add(left, right):
        return (left.astype(F32) + right.astype(F32)).astype(BF16)

    returned = lax.all_to_all(back, ("dp", "table"), 0, 0, tiled=True)
    parts = []
    for side, seq in enumerate((seq_a, seq_b)):
        keep, send = pairs[2 * side], pairs[2 * side + 1]
        for place, bit in enumerate(seq):
            taken = exchange(send, "dp", 1 << bit)
            if place < len(seq) - 1:
                mid = keep.shape[0] // 2
                send = add(keep[mid:], taken[mid:])
                keep = add(keep[:mid], taken[:mid])
        for low in range(0, half, size):
            parts.append(add(keep[0, :, low : low + size], taken[0, :, low : low + size]))
    parts = jnp.stack(parts)
    own = [lax.dynamic_index_in_dim(parts, plane ^ m, 0, False) for m in range(planes)]
    total = own[0].astype(F32)
    for m in range(1, planes):
        total = total + exchange(own[m], "table", m).astype(F32)
    summed = total.astype(BF16)
    whole = [summed]
    for m in range(1, planes):
        whole.append(exchange(summed, "table", m))
    grad_proj, grad_in, grad_out = pl.pallas_call(
        functools.partial(join_kernel, planes, width),
        out_shape=(
            jax.ShapeDtypeStruct((rows_each, width), F32),
            jax.ShapeDtypeStruct((rows_each, 4 * width), F32),
            jax.ShapeDtypeStruct((rows_each, width), F32),
        ),
        in_specs=[SM] + [VM] * planes,
        out_specs=(VM,) * 3,
        scratch_shapes=[pltpu.VMEM((rows_each, 2 * half), F32)],
        compiler_params=params(6),
        name="join",
    )(me, *whole)
    g_a, g_b, g_c, g_d = pl.pallas_call(
        functools.partial(scatter_kernel, devices, capacity, row_counts, widths),
        out_shape=(
            jax.ShapeDtypeStruct((widths[0], row_counts[0]), BF16),
            jax.ShapeDtypeStruct((widths[1], row_counts[1]), BF16),
            jax.ShapeDtypeStruct((row_counts[2], widths[2]), BF16),
            jax.ShapeDtypeStruct((row_counts[3], widths[3]), BF16),
        ),
        in_specs=[VM] * 3,
        out_specs=(HB,) * 4,
        scratch_shapes=[
            pltpu.VMEM((widths[0], row_counts[0]), BF16),
            pltpu.VMEM((widths[1], row_counts[1]), BF16),
            pltpu.VMEM((row_counts[2], widths[2]), BF16),
            pltpu.VMEM((row_counts[3], widths[3]), BF16),
            pltpu.VMEM((4, slots + 8, 128), F32),
            pltpu.VMEM((devices + 1, 4 * capacity, 128), F32),
            pltpu.SemaphoreType.DMA((4,)),
        ],
        compiler_params=params(26),
        name="scatter",
    )(returned, idxc, idxr)
    return output, g_a.T, g_b.T, g_c, g_d, grad_proj, grad_in, grad_out


def solution(mesh):
    both = ("dp", "table")
    return jax.shard_map(
        step,
        mesh=mesh,
        in_specs=(
            P(both, None), P(both, None), P(both), P(both),
            P(both, None), P(both, None), P(both, None), P(both, None),
            P("dp", None), P("dp", None), P("dp", None), P(both, None, None),
        ),
        out_specs=(
            P(both, None, None), P(both, None), P(both, None), P(both, None), P(both, None),
            P("dp", None), P("dp", None), P("dp", None),
        ),
        check_vma=False,
    )
```
